128 devices in a mesh: dp: 4 (over z), fsdp: 32 (over y, x, core).
Axes of the slice: x: 4, y: 4, z: 4, core: 2. Of those that a mesh axis runs over, the one named last changes fastest.
Arguments:
- logged: bfloat16 [2048, 8192], P('dp', 'fsdp'), may hold values from -6 to 6
- pairs: int32 [512, 2], P('dp'), may hold values from 0 to 511
- clicks: int32 [512], P('dp'), may hold values 0 or 1
- query_pairs: int32 [32, 2], P('dp'), may hold values from 0 to 511
- query_clicks: int32 [32], P('dp'), may hold values 0 or 1
- first_weight: bfloat16 [8192, 8192], P(None, 'fsdp'), may hold values from -0.0625 to 0.0625
- second_weight: bfloat16 [8192, 8192], P(None, 'fsdp'), may hold values from -0.0625 to 0.0625
- head_weight: float32 [8192], P('fsdp'), may hold values from -0.0625 to 0.0625
Outputs:
- solution: float32 [8192, 8192], P('dp', 'fsdp')
- influence: float32 [512], P('dp')
The draws below stay inside these ranges and needn't reach their ends.
Inputs may be any that keep to these rules, and one draw needn't show every extreme that they name: Each block of 128 pairs indexes rows within the matching block of 512 logged rows. `query_pairs`: each block of 8 query pairs indexes rows within the matching block of 512 logged rows.
All inputs are finite; a program needn't handle non-finite values. No bound on the sum of `clicks` or of `query_clicks` on one device may be relied on, other than what follows from the above.
Results may differ from the reference program's by a relative error of at most 0.035.
Values may be sent and summed in bfloat16 or wider, within the bound.
A program may use at most 128 MiB of HBM per device.

```python
import jax
import jax.numpy as jnp
from jax import lax

D = 8192
PAIRS = 128
QPAIRS = 8
TABLE_DEV = 512
ALL_PAIRS = 512
ALL_QUERIES = 32
TABLE = 2048
N_FSDP = 32


def with_ends(values, rng, low, high):
    index_at = [jax.random.randint(jax.random.fold_in(rng, axis), (), 0, length) for axis, length in enumerate(values.shape)]
    widest = values.shape.index(max(values.shape))
    next_to = index_at[:widest] + [(index_at[widest] + 1) % values.shape[widest]] + index_at[widest + 1:]
    return values.at[tuple(index_at)].set(low).at[tuple(next_to)].set(high)


def block_scale(stream_key, shape, split, low, largest):
    factor_of = 1.0
    for dim, blocks in split:
        steps = jax.random.uniform(jax.random.fold_in(jax.random.fold_in(stream_key, 6), dim), (blocks,), jnp.float32, low / len(split), largest / len(split))
        factor_of = factor_of * jnp.repeat(jnp.exp(steps), shape[dim] // blocks).reshape((-1,) + (1,) * (len(shape) - 1 - dim))
    return factor_of


def noise(stream_key, dims, spread, limit, cuts=(), dtype=jnp.bfloat16):
    factor_of = block_scale(stream_key, dims, cuts, -0.22, 0.18) if cuts else 1.0
    entries = jax.random.normal(stream_key, dims, jnp.float32) * spread * factor_of
    return jnp.minimum(jnp.maximum(entries, -limit), limit).astype(dtype)


def setup_inputs(seed: int = 0) -> dict:
    streams_of = jax.random.split(jax.random.key(seed), 9)
    return {
        "logged": noise(streams_of[0], (TABLE, D), 1.0, 6.0, ((0, 4), (1, 32))),
        "pairs": with_ends(jax.random.randint(streams_of[1], (ALL_PAIRS, 2), 0, TABLE_DEV), jax.random.fold_in(streams_of[1], 1), 0, TABLE_DEV - 1).astype(jnp.int32),
        "clicks": with_ends((jax.random.randint(streams_of[2], (ALL_PAIRS,), 0, 2) < 1).astype(jnp.int32), jax.random.fold_in(streams_of[2], 1), 0, 1),
        "query_pairs": with_ends(jax.random.randint(streams_of[3], (ALL_QUERIES, 2), 0, TABLE_DEV), jax.random.fold_in(streams_of[3], 1), 0, TABLE_DEV - 1).astype(jnp.int32),
        "query_clicks": with_ends((jax.random.randint(streams_of[4], (ALL_QUERIES,), 0, 2) < 1).astype(jnp.int32), jax.random.fold_in(streams_of[4], 1), 0, 1),
        "first_weight": noise(streams_of[5], (D, D), D ** -0.5, 0.0625, ((1, 32),)),
        "second_weight": noise(streams_of[6], (D, D), D ** -0.5, 0.0625, ((1, 32),)),
        "head_weight": noise(streams_of[7], (D,), D ** -0.5, 0.0625, ((0, 32),), jnp.float32),
    }


DAMPING = 0.01


def back_project(coef, second_weight):
    width = D // N_FSDP
    blocks_coef = coef.reshape(coef.shape[0], N_FSDP, width).transpose(1, 0, 2)
    blocks_weight = second_weight.reshape(D, N_FSDP, width).transpose(1, 0, 2)

    def add_block(carry, pieces):
        term = jnp.dot(pieces[0], pieces[1].T, preferred_element_type=jnp.float32)
        term = lax.optimization_barrier(term.astype(jnp.bfloat16))
        return carry + term.astype(jnp.float32), None

    start_zero = jnp.zeros((coef.shape[0], D), jnp.float32)
    return lax.scan(add_block, start_zero, (blocks_coef, blocks_weight))[0]


def pair_terms(first_score, second_score, outcome):
    signed = 2.0 * outcome.astype(jnp.float32) - 1.0
    margin = first_score - second_score
    slope_term = -signed * jax.nn.sigmoid(-signed * margin)
    curve_term = jax.nn.sigmoid(signed * margin) * jax.nn.sigmoid(-signed * margin)
    return slope_term, curve_term


def reference(logged, pairs, clicks, query_pairs, query_clicks, first_weight, second_weight, head_weight):
    pair_base = (jnp.arange(ALL_PAIRS) // PAIRS * TABLE_DEV).astype(jnp.int32)
    query_base = (jnp.arange(ALL_QUERIES) // QPAIRS * TABLE_DEV).astype(jnp.int32)
    row_ids = jnp.concatenate([pairs[:, 0] + pair_base, pairs[:, 1] + pair_base,
                               query_pairs[:, 0] + query_base, query_pairs[:, 1] + query_base]).astype(jnp.int32)
    feats = logged[row_ids]
    hidden = jnp.tanh(jnp.dot(feats, first_weight, preferred_element_type=jnp.float32)).astype(jnp.bfloat16)
    output_act = jnp.tanh(jnp.dot(hidden, second_weight, preferred_element_type=jnp.float32))
    scores_all = jnp.sum(output_act * head_weight, axis=1)
    coef = (head_weight * (1.0 - output_act * output_act)).astype(jnp.bfloat16)
    back = back_project(coef, second_weight)
    hidden_float = hidden.astype(jnp.float32)
    mixing = (1.0 - hidden_float * hidden_float) * back
    count = 2 * ALL_PAIRS
    slope_train, curve_train = pair_terms(scores_all[:ALL_PAIRS], scores_all[ALL_PAIRS:count], clicks)
    slope_query = pair_terms(scores_all[count:count + ALL_QUERIES], scores_all[count + ALL_QUERIES:], query_clicks)[0]
    query_err = jnp.concatenate([slope_query, -slope_query])
    query_rows = (query_err[:, None] * mixing[count:]).astype(jnp.bfloat16)
    gradient = jnp.dot(feats[count:].T, query_rows, preferred_element_type=jnp.float32)
    train_feats = feats[:count]
    train_mix = mixing[:count]

    def apply_curvature(direction):
        packed = direction.astype(jnp.bfloat16)
        project = jnp.dot(train_feats, packed, preferred_element_type=jnp.float32)
        response = jnp.sum(train_mix * project, axis=1)
        rdiff = response[:ALL_PAIRS] - response[ALL_PAIRS:]
        resp_err = jnp.concatenate([curve_train * rdiff, -curve_train * rdiff])
        resp_rows = (resp_err[:, None] * train_mix).astype(jnp.bfloat16)
        product = jnp.dot(train_feats.T, resp_rows, preferred_element_type=jnp.float32)
        return packed, product, rdiff

    norm_first = jnp.sum(gradient * gradient)
    packed_first, product_first, rdiff_first = apply_curvature(gradient)
    curv_first = jnp.sum(packed_first.astype(jnp.float32) * product_first) + DAMPING * norm_first
    alpha_first = norm_first / curv_first
    residual_next = gradient - alpha_first * (product_first + DAMPING * gradient)
    norm_next = jnp.sum(residual_next * residual_next)
    direction_next = residual_next + (norm_next / norm_first) * gradient
    packed_next, product_next, rdiff_next = apply_curvature(direction_next)
    curv_next = jnp.sum(packed_next.astype(jnp.float32) * product_next) + DAMPING * jnp.sum(direction_next * direction_next)
    alpha_next = norm_next / curv_next
    solution = alpha_first * gradient + alpha_next * direction_next
    influence = -slope_train * (alpha_first * rdiff_first + alpha_next * rdiff_next)
    return solution, influence
```

```python
import jax
import jax.numpy as jnp
from jax import lax
from jax.experimental import pallas as pl
from jax.experimental.pallas import tpu as pltpu
from jax.sharding import PartitionSpec as P

DAMPING = 0.01
MESH = pl.DeviceIdType.MESH
F32 = jnp.float32
BF16 = jnp.bfloat16

NP = 128
NT = 256
NQ = 16
ROWS = 272
W = 256


def dot(left, right):
    return jnp.dot(left, right, preferred_element_type=F32)


def dot_nt(left, right):
    return lax.dot_general(left, right, (((1,), (1,)), ((), ())), preferred_element_type=F32)


def kernel(
    logged, pairs, clicks, qpairs, qclicks, w1, w2, head,
    out, infl,
    Fg, Hg, W1o, W1s, W2o, W2s, Ao, As, Ar, Bs, Br, Co, Cs, Pb, RB, Sa, RA, Fz, FT, FU,
    MX, QA, SC, SCr, SP, SPr, SZ, Gf, Gp, Pf, Pp, R0, AR, ARr, ARp, ARpr, ARz,
    loc, wsnd, wrcv, asnd, arcv, bsnd, brcv, csnd, crcv, dsnd, drcv, fsnd, frcv, gsnd, grcv,
    msnd, mrcv, ssnd, srcv, rsnd, rrcv,
):
    z = lax.axis_index("dp")
    f = lax.axis_index("fsdp")
    c = lax.rem(f, 2)
    me = lax.div(f, 2)
    x = lax.rem(me, 4)
    y = lax.div(me, 4)

    def plane(da, db):
        nx = lax.rem(x + da * (1 - c) + db * c + 8, 4)
        ny = lax.rem(y + da * c + db * (1 - c) + 8, 4)
        return ny * 4 + nx

    def dev(da, db):
        return (z, plane(da, db) * 2 + c)

    def zdev(dz):
        return (lax.rem(z + dz + 4, 4), f)

    sibling = (z, me * 2 + 1 - c)
    offsets = [(da, db) for da in range(4) for db in range(4) if (da, db) != (0, 0)]
    partners = [sibling] + [dev(da, db) for da, db in offsets] + [zdev(d) for d in (1, 2, 3)]
    barrier = pltpu.get_barrier_semaphore()
    for partner in partners:
        pl.semaphore_signal(barrier, inc=1, device_id=partner, device_id_type=MESH)
    pl.semaphore_wait(barrier, len(partners))

    sent = []

    def remote(src, dst, send_sem, recv_sem, device):
        return pltpu.make_async_remote_copy(
            src_ref=src, dst_ref=dst, send_sem=send_sem, recv_sem=recv_sem,
            device_id=device, device_id_type=MESH,
        )

    def push(src, dst, send_sem, recv_sem, device):
        copy = remote(src, dst, send_sem, recv_sem, device)
        copy.start()
        sent.append(copy)
        return copy

    w1_own = pltpu.make_async_copy(w1.at[:, c], W1o, loc.at[0])
    w2_own = pltpu.make_async_copy(w2.at[:, c], W2o, loc.at[1])
    w1_own.start()
    w1_sib = push(w1.at[:, 1 - c], W1s, wsnd.at[0], wrcv.at[0], sibling)

    table = logged[...]

    def select(ids):
        lanes = lax.broadcasted_iota(jnp.int32, (ids.shape[0], 512), 1)
        return dot((ids == lanes).astype(F32).astype(BF16), table).astype(BF16)

    Fg[me, 0:NP] = select(pairs[:, 0:1])
    Fg[me, NP:NT] = select(pairs[:, 1:2])
    Fg[me, NT:ROWS] = select(jnp.concatenate([qpairs[:, 0:1], qpairs[:, 1:2]], axis=0))

    def gather_matmul(buf, wo, ws, snd, rcv, ready, acc_o, acc_s):
        first = {}
        for d in (2, 1, 3):
            first[d] = push(buf.at[me], buf.at[me], snd.at[d - 1], rcv.at[d - 1], dev(d, 0))
        for e in (2, 1, 3):
            push(buf.at[me], buf.at[me], snd.at[2 + e], rcv.at[2 + e], dev(0, e))
        ready()
        block = buf[me]
        acc_o[...] = dot(block, wo[me])
        acc_s[...] = dot(block, ws[me])
        for d in (1, 3, 2):
            first[d].wait_recv()
            slot = plane(-d, 0)
            for e in (2, 1, 3):
                push(buf.at[slot], buf.at[slot], snd.at[3 * d + 2 + e], rcv.at[3 * d + 2 + e], dev(0, e))

        @pl.loop(1, 4)
        def _(d):
            slot = plane(-d, 0)
            block = buf[slot]
            acc_o[...] += dot(block, wo[slot])
            acc_s[...] += dot(block, ws[slot])

        @pl.loop(0, 12)
        def _(i):
            slot = plane(-lax.div(i, 3), -(lax.rem(i, 3) + 1))
            remote(buf.at[slot], buf.at[slot], snd.at[3 + i], rcv.at[3 + i], sibling).wait_recv()
            block = buf[slot]
            acc_o[...] += dot(block, wo[slot])
            acc_s[...] += dot(block, ws[slot])

    def w1_ready():
        w2_own.start()
        w1_own.wait()
        w1_sib.wait_recv()

    gather_matmul(Fg, W1o, W1s, asnd, arcv, w1_ready, Ao, As)
    acc_copy = push(As, Ar, dsnd.at[0], drcv.at[0], sibling)
    w2_sib = push(w2.at[:, 1 - c], W2s, wsnd.at[1], wrcv.at[1], sibling)
    acc_copy.wait_recv()
    hidden = jnp.tanh(Ao[...] + Ar[...]).astype(BF16)
    Hg[me] = hidden

    def w2_ready():
        for dz in (1, 2, 3):
            z2 = lax.rem(z + dz, 4)
            fz_copies[dz] = push(
                Fg.at[pl.ds(4 * z2, 4)], Fz.at[z, c], fsnd.at[dz - 1], frcv.at[dz - 1], zdev(dz)
            )
        own = Fg.at[pl.ds(4 * z, 4)]
        fz_own.append(pltpu.make_async_copy(own, Fz.at[z, c], loc.at[2]))
        fz_own[0].start()
        fz_sib.append(push(own, Fz.at[z, c], gsnd.at[0], grcv.at[0], sibling))
        w2_own.wait()
        w2_sib.wait_recv()

    fz_copies, fz_own, fz_sib = {}, [], []
    gather_matmul(Hg, W2o, W2s, bsnd, brcv, w2_ready, Ao, Bs)
    acc_copy = push(Bs, Br, dsnd.at[1], drcv.at[1], sibling)
    acc_copy.wait_recv()
    act = jnp.tanh(Ao[...] + Br[...])
    weights = head[...]
    Co[...] = (weights * (1.0 - act * act)).astype(BF16)
    coef_copy = push(Co, Cs, dsnd.at[2], drcv.at[2], sibling)

    rows128 = lax.broadcasted_iota(jnp.int32, (128, 128), 0)
    lanes128 = lax.broadcasted_iota(jnp.int32, (128, 128), 1)
    eye = rows128 == lanes128

    def to_row(column):
        return jnp.sum(jnp.where(eye, jnp.broadcast_to(column, (128, 128)), 0.0), axis=0, keepdims=True)

    def to_column(row):
        return jnp.sum(jnp.where(eye, jnp.broadcast_to(row, (128, 128)), 0.0), axis=1, keepdims=True)

    part = jnp.sum(act * weights, axis=1, keepdims=True)
    SC[...] = jnp.zeros((8, 128), F32)
    SC[0:1] = to_row(part[0:NP])
    SC[1:2] = to_row(part[NP:NT])
    SC[2:3] = to_row(jnp.concatenate([part[NT:ROWS], jnp.zeros((128 - NQ, 1), F32)], axis=0))
    score_pair = push(SC, SCr, dsnd.at[3], drcv.at[3], sibling)

    coef_copy.wait_recv()

    def back_block(k):
        return dot_nt(Co[...], W2o[k]) + dot_nt(Cs[...], W2s[k])

    order = (2, 1, 3, 0)
    rb = {}
    for da in order:
        for e in (2, 1, 3):
            k = plane(da, e)
            Pb[k] = back_block(k).astype(BF16)
            i = 3 * da + e - 1
            rb[da, e] = push(Pb.at[k], RB.at[i], csnd.at[i], crcv.at[i], dev(0, e))
    score_pair.wait_recv()
    SP[...] = SC[...] + SCr[...]
    sp = [
        push(SP, SPr.at[i], ssnd.at[i], srcv.at[i], dev(da, db)) for i, (da, db) in enumerate(offsets)
    ]
    for da in order:
        Sa[da] = back_block(plane(da, 0))
    ra = {}
    for da in order:
        total = Sa[da]
        for e in (1, 3, 2):
            rb[da, e].wait_recv()
            total += RB[3 * da + e - 1].astype(F32)
        Sa[da] = total
        if da:
            Pb[plane(da, 0)] = total.astype(BF16)
            ra[da] = push(
                Pb.at[plane(da, 0)], RA.at[da - 1], csnd.at[11 + da], crcv.at[11 + da], dev(da, 0)
            )
    score = SP[...]
    for i, copy in enumerate(sp):
        copy.wait_recv()
        score += SPr[i]
    SZ[0] = score
    sz = [push(SZ.at[0], SZ.at[d], ssnd.at[14 + d], srcv.at[14 + d], zdev(d)) for d in (1, 2, 3)]

    for dz in (1, 3, 2):
        fz_copies[dz].wait_recv()
        zs = lax.rem(z - dz + 4, 4)
        fz_sib.append(push(Fz.at[zs, c], Fz.at[zs, c], gsnd.at[dz], grcv.at[dz], sibling))
    fz_own[0].wait()

    def transpose_half(par):
        @pl.loop(0, 4)
        def _(k):
            for zz in range(4):
                FT[par, k, :, zz * NT : (zz + 1) * NT] = Fz[zz, par, k, 0:NT].T
            queries = jnp.concatenate([Fz[zz, par, k, NT:ROWS] for zz in range(4)], axis=0)
            FU[par, k] = queries.astype(F32).T.astype(BF16)

    for copy in fz_sib:
        copy.wait_recv()
    transpose_half(0)
    transpose_half(1)

    total = Sa[0]
    for d in (1, 3, 2):
        ra[d].wait_recv()
        total += RA[d - 1].astype(F32)
    own_hidden = Hg[me].astype(F32)
    mixing = (1.0 - own_hidden * own_hidden) * total

    margin = score[2:3] - pltpu.roll(score[2:3], 120, 1)
    signed = 2.0 * qclicks[...].astype(F32) - 1.0
    slope_query = -signed * jax.nn.sigmoid(-signed * margin[:, 0:8])
    err_row = jnp.concatenate([slope_query, -slope_query, jnp.zeros((1, 112), F32)], axis=1)
    err = to_column(err_row)[0:NQ]
    QA[z] = (err * mixing[NT:ROWS]).astype(BF16)
    qa = [push(QA.at[z], QA.at[z], msnd.at[d - 1], mrcv.at[d - 1], zdev(d)) for d in (1, 2, 3)]
    MX[z] = mixing[0:NT].astype(BF16)
    mx = [push(MX.at[z], MX.at[z], msnd.at[2 + d], mrcv.at[2 + d], zdev(d)) for d in (1, 2, 3)]

    for copy in sz:
        copy.wait_recv()
    train_margin = []
    for zz in range(4):
        tile = SZ[lax.rem(z - zz + 4, 4)]
        train_margin.append(tile[0:1] - tile[1:2])
    margins = jnp.concatenate(train_margin, axis=0)
    curve = jax.nn.sigmoid(margins) * jax.nn.sigmoid(-margins)

    for copy in qa:
        copy.wait_recv()
    squares = jnp.zeros((1, W), F32)
    query_rows = jnp.concatenate([QA[zz] for zz in range(4)], axis=0)
    for par in range(2):
        for k in range(4):
            block = dot(FU[par, k], query_rows)
            squares += jnp.sum(block * block, axis=0, keepdims=True)
            Gf[par, k] = block
            Gp[par, k] = block.astype(BF16)
    for copy in mx:
        copy.wait_recv()

    def responses(direction):
        first, second = [], []
        for zz in range(4):
            project = jnp.zeros((NT, W), F32)
            for par in range(2):
                for k in range(4):
                    project += dot(Fz[zz, par, k, 0:NT], direction[par, k])
            column = jnp.sum(MX[zz].astype(F32) * project, axis=1, keepdims=True)
            first.append(to_row(column[0:NP]))
            second.append(to_row(column[NP:NT]))
        return jnp.concatenate(first + second, axis=0)

    def all_reduce(tile, turn):
        base = turn * 19
        AR[turn] = tile
        pair = push(AR.at[turn], ARr.at[turn], rsnd.at[base], rrcv.at[base], sibling)
        pair.wait_recv()
        tile = AR[turn] + ARr[turn]
        ARp[turn] = tile
        copies = [
            push(ARp.at[turn], ARpr.at[turn, i], rsnd.at[base + 1 + i], rrcv.at[base + 1 + i], dev(da, db))
            for i, (da, db) in enumerate(offsets)
        ]
        for i, copy in enumerate(copies):
            copy.wait_recv()
            tile += ARpr[turn, i]
        ARz[turn, 0] = tile
        copies = [
            push(ARz.at[turn, 0], ARz.at[turn, d], rsnd.at[base + 15 + d], rrcv.at[base + 15 + d], zdev(d))
            for d in (1, 2, 3)
        ]
        for d, copy in enumerate(copies):
            copy.wait_recv()
            tile += ARz[turn, d + 1]
        return tile

    norm_part = jnp.broadcast_to(jnp.sum(squares, axis=1, keepdims=True), (8, 128))
    tile = all_reduce(jnp.concatenate([responses(Gp), norm_part], axis=0), 0)
    rdiff_first = tile[0:4] - tile[4:8]
    norm_first = tile[8:9, 0:1]
    resp_err = curve * rdiff_first
    for zz in range(4):
        scale = to_column(resp_err[zz : zz + 1])
        R0[zz * NT : zz * NT + NP] = (scale * MX[zz, 0:NP].astype(F32)).astype(BF16)
        R0[zz * NT + NP : (zz + 1) * NT] = (-scale * MX[zz, NP:NT].astype(F32)).astype(BF16)
    for par in range(2):
        for k in range(4):
            block = dot(FT[par, k], R0[...])
            Pf[par, k] = block
            Pp[par, k] = block.astype(BF16)
    tile = all_reduce(jnp.concatenate([responses(Pp), norm_part], axis=0), 1)
    rdiff_prod = tile[0:4] - tile[4:8]

    def total_of(value):
        return jnp.sum(jnp.sum(value, axis=1, keepdims=True), axis=0, keepdims=True)

    cross = total_of(curve * rdiff_first * rdiff_first)
    prod_norm = total_of(curve * rdiff_first * rdiff_prod)
    curv_first = cross + DAMPING * norm_first
    alpha_first = norm_first / curv_first
    keep = 1.0 - DAMPING * alpha_first
    norm_next = keep * keep * norm_first - 2.0 * keep * alpha_first * cross + alpha_first * alpha_first * prod_norm
    lead = keep + norm_next / norm_first
    rdiff_next = lead * rdiff_first - alpha_first * rdiff_prod
    direction_norm = lead * lead * norm_first - 2.0 * lead * alpha_first * cross + alpha_first * alpha_first * prod_norm
    curv_next = total_of(curve * rdiff_next * rdiff_next) + DAMPING * direction_norm
    alpha_next = norm_next / curv_next
    on_gradient = alpha_first + alpha_next * lead
    on_product = -alpha_next * alpha_first
    for par in range(2):
        for k in range(4):
            row = (2 * k + par) * W
            out[row : row + W] = on_gradient * Gf[par, k] + on_product * Pf[par, k]

    own_margin = score[0:1] - score[1:2]
    signed = 2.0 * clicks[...].astype(F32) - 1.0
    slope = -signed * jax.nn.sigmoid(-signed * own_margin)
    mine = lax.broadcasted_iota(jnp.int32, (4, 128), 0) == z
    change = alpha_first * rdiff_first + alpha_next * rdiff_next
    infl[...] = -slope * jnp.sum(jnp.where(mine, change, 0.0), axis=0, keepdims=True)

    for copy in sent:
        copy.wait_send()


def local(logged, pairs, clicks, query_pairs, query_clicks, first_weight, second_weight, head_weight):
    vmem = pl.BlockSpec(memory_space=pltpu.VMEM)
    hbm = pl.BlockSpec(memory_space=pl.ANY)
    V = pltpu.VMEM
    dma = pltpu.SemaphoreType.DMA
    block = (ROWS, W)
    scratch = [
        V((16, *block), BF16), V((16, *block), BF16),
        V((16, W, W), BF16), V((16, W, W), BF16), V((16, W, W), BF16), V((16, W, W), BF16),
        V(block, F32), V(block, F32), V(block, F32), V(block, F32), V(block, F32),
        V(block, BF16), V(block, BF16),
        V((16, *block), BF16), V((12, *block), BF16), V((4, *block), F32), V((3, *block), BF16),
        V((4, 2, 4, *block), BF16), V((2, 4, W, 4 * NT), BF16), V((2, 4, W, 4 * NQ), BF16),
        V((4, NT, W), BF16), V((4, NQ, W), BF16),
        V((8, 128), F32), V((8, 128), F32), V((8, 128), F32), V((15, 8, 128), F32), V((4, 8, 128), F32),
        V((2, 4, W, W), F32), V((2, 4, W, W), BF16), V((2, 4, W, W), F32), V((2, 4, W, W), BF16),
        V((4 * NT, W), BF16),
        V((2, 16, 128), F32), V((2, 16, 128), F32), V((2, 16, 128), F32),
        V((2, 15, 16, 128), F32), V((2, 4, 16, 128), F32),
        dma((3,)),
        dma((2,)), dma((2,)), dma((15,)), dma((15,)), dma((15,)), dma((15,)), dma((15,)), dma((15,)),
        dma((4,)), dma((4,)), dma((3,)), dma((3,)), dma((4,)), dma((4,)),
        dma((6,)), dma((6,)), dma((18,)), dma((18,)), dma((38,)), dma((38,)),
    ]
    solved, influence = pl.pallas_call(
        kernel,
        out_shape=(jax.ShapeDtypeStruct((2048, W), F32), jax.ShapeDtypeStruct((1, NP), F32)),
        in_specs=[vmem, vmem, vmem, vmem, vmem, hbm, hbm, vmem],
        out_specs=(vmem, vmem),
        scratch_shapes=scratch,
        compiler_params=pltpu.CompilerParams(
            collective_id=0, has_side_effects=True, vmem_limit_bytes=60 << 20
        ),
    )(
        logged,
        pairs,
        clicks.reshape(1, NP),
        query_pairs,
        query_clicks.reshape(1, 8),
        first_weight.reshape(16, 2, W, W),
        second_weight.reshape(16, 2, W, W),
        head_weight.reshape(1, W),
    )
    return (solved, influence.reshape(NP))


def solution(mesh):
    placed = (
        P("dp", "fsdp"),
        P("dp", None),
        P("dp"),
        P("dp", None),
        P("dp"),
        P(None, "fsdp"),
        P(None, "fsdp"),
        P("fsdp"),
    )
    return jax.shard_map(
        local, mesh=mesh, in_specs=placed, out_specs=(P("dp", "fsdp"), P("dp")), check_vma=False
    )
```

```python
import jax
import jax.numpy as jnp
from jax import lax
from jax.experimental import pallas as pl
from jax.experimental.pallas import tpu as pltpu
from jax.sharding import PartitionSpec as P

DAMPING = 0.01
MESH = pl.DeviceIdType.MESH
F32 = jnp.float32
BF16 = jnp.bfloat16

NP = 128
NQ = 16
HALF = (144, 128)
W = 256


def dot(left, right):
    return jnp.dot(left, right, preferred_element_type=F32)


def dot_nt(left, right):
    return lax.dot_general(left, right, (((1,), (1,)), ((), ())), preferred_element_type=F32)


def kernel(
    logged, pairs, clicks, qpairs, qclicks, w1, w2, head,
    g_out, p_out, on_g, on_p, infl,
    F0, F1, H0, H1, W1o, W1s, W2o, W2s,
    Ao0, Ao1, As0, As1, Ar0, Ar1, Bo0, Bo1, Bs0, Bs1, Br0, Br1,
    Co0, Co1, Cs0, Cs1, Pb0, Pb1, RB0, RB1, Sa0, Sa1, RA0, RA1,
    Fz0, Fz1, FT, FU, KT, MX, QA, SC, SCr, SP, SPr, SZ, Gf, Pf, Pp, R0,
    AR, ARr, ARp, ARpr, ARz,
    loc, wsnd, wrcv, asnd, arcv, bsnd, brcv, csnd, crcv, dsnd, drcv, fsnd, frcv, gsnd, grcv,
    ksnd, krcv, msnd, mrcv, ssnd, srcv, rsnd, rrcv,
):
    F, H = (F0, F1), (H0, H1)
    Ao, As, Ar = (Ao0, Ao1), (As0, As1), (Ar0, Ar1)
    Bo, Bs, Br = (Bo0, Bo1), (Bs0, Bs1), (Br0, Br1)
    Co, Cs = (Co0, Co1), (Cs0, Cs1)
    Pb, RB, Sa, RA = (Pb0, Pb1), (RB0, RB1), (Sa0, Sa1), (RA0, RA1)
    Fz = (Fz0, Fz1)

    z = lax.axis_index("dp")
    f = lax.axis_index("fsdp")
    c = lax.rem(f, 2)
    me = lax.div(f, 2)
    x = lax.rem(me, 4)
    y = lax.div(me, 4)

    def plane(da, db):
        nx = lax.rem(x + da * (1 - c) + db * c + 8, 4)
        ny = lax.rem(y + da * c + db * (1 - c) + 8, 4)
        return ny * 4 + nx

    def dev(da, db):
        return (z, plane(da, db) * 2 + c)

    def zdev(dz):
        return (lax.rem(z + dz + 4, 4), f)

    sibling = (z, me * 2 + 1 - c)
    offsets = [(da, db) for da in range(4) for db in range(4) if (da, db) != (0, 0)]
    partners = [sibling] + [dev(da, db) for da, db in offsets] + [zdev(d) for d in (1, 2, 3)]
    barrier = pltpu.get_barrier_semaphore()
    for partner in partners:
        pl.semaphore_signal(barrier, inc=1, device_id=partner, device_id_type=MESH)
    pl.semaphore_wait(barrier, len(partners))

    sent = []

    def remote(src, dst, send_sem, recv_sem, device):
        return pltpu.make_async_remote_copy(
            src_ref=src, dst_ref=dst, send_sem=send_sem, recv_sem=recv_sem,
            device_id=device, device_id_type=MESH,
        )

    def push(src, dst, send_sem, recv_sem, device):
        copy = remote(src, dst, send_sem, recv_sem, device)
        copy.start()
        sent.append(copy)
        return copy

    rows128 = lax.broadcasted_iota(jnp.int32, (128, 128), 0)
    lanes128 = lax.broadcasted_iota(jnp.int32, (128, 128), 1)
    eye = rows128 == lanes128

    def to_row(column):
        return jnp.sum(jnp.where(eye, jnp.broadcast_to(column, (128, 128)), 0.0), axis=0, keepdims=True)

    def to_column(row):
        return jnp.sum(jnp.where(eye, jnp.broadcast_to(row, (128, 128)), 0.0), axis=1, keepdims=True)

    w1_own = pltpu.make_async_copy(w1.at[:, c], W1o, loc.at[0])
    w2_own = pltpu.make_async_copy(w2.at[:, c], W2o, loc.at[1])
    w1_own.start()
    w1_sib = push(w1.at[:, 1 - c], W1s, wsnd.at[0], wrcv.at[0], sibling)

    def gather_send(h, buf, snd, rcv):
        first = {}
        for d in (2, 1, 3):
            first[d] = push(buf[h].at[me], buf[h].at[me], snd.at[h, d - 1], rcv.at[h, d - 1], dev(d, 0))
        for e in (2, 1, 3):
            push(buf[h].at[me], buf[h].at[me], snd.at[h, 2 + e], rcv.at[h, 2 + e], dev(0, e))
        return first

    def gather_forward(h, buf, snd, rcv, first):
        for d in (1, 3, 2):
            first[d].wait_recv()
            slot = plane(-d, 0)
            for e in (2, 1, 3):
                i = 3 * d + 2 + e
                push(buf[h].at[slot], buf[h].at[slot], snd.at[h, i], rcv.at[h, i], dev(0, e))

    def matmul_head(h, buf, wo, ws, acc_o, acc_s):
        block = buf[h][me]
        acc_o[h][...] = dot(block, wo[me])
        acc_s[h][...] = dot(block, ws[me])

        @pl.loop(1, 4)
        def _(d):
            slot = plane(-d, 0)
            block = buf[h][slot]
            acc_o[h][...] += dot(block, wo[slot])
            acc_s[h][...] += dot(block, ws[slot])

    def matmul_tail(h, buf, wo, ws, acc_o, acc_s, snd, rcv):
        @pl.loop(0, 12)
        def _(i):
            slot = plane(-lax.div(i, 3), -(lax.rem(i, 3) + 1))
            remote(buf[h].at[slot], buf[h].at[slot], snd.at[h, 3 + i], rcv.at[h, 3 + i], sibling).wait_recv()
            block = buf[h][slot]
            acc_o[h][...] += dot(block, wo[slot])
            acc_s[h][...] += dot(block, ws[slot])

    def select(row, count):
        lanes = lax.broadcasted_iota(jnp.int32, (128, 512), 1)
        ids = to_column(row.astype(F32)).astype(jnp.int32)
        return dot((ids == lanes).astype(F32).astype(BF16)[0:count], logged[...]).astype(BF16)

    F0[me, 0:NP] = select(pairs[0:1], NP)
    query_ids = jnp.concatenate([qpairs[0:1], qpairs[1:2], jnp.zeros((1, 112), jnp.int32)], axis=1)
    F0[me, NP:144] = select(query_ids, NQ)
    first0 = gather_send(0, F, asnd, arcv)
    F1[me] = select(pairs[1:2], NP)
    first1 = gather_send(1, F, asnd, arcv)
    gather_forward(0, F, asnd, arcv, first0)
    gather_forward(1, F, asnd, arcv, first1)
    w1_own.wait()
    w1_sib.wait_recv()
    w2_own.start()
    w2_sib = push(w2.at[:, 1 - c], W2s, wsnd.at[1], wrcv.at[1], sibling)

    fz_copies, fz_own, fz_sib = {}, {}, []

    def feature_exchange(h):
        for dz in (1, 3, 2):
            z2 = lax.rem(z + dz, 4)
            fz_copies[h, dz] = push(
                F[h].at[pl.ds(4 * z2, 4)], Fz[h].at[z, c], fsnd.at[h, dz - 1], frcv.at[h, dz - 1], zdev(dz)
            )
        own = F[h].at[pl.ds(4 * z, 4)]
        fz_own[h] = pltpu.make_async_copy(own, Fz[h].at[z, c], loc.at[2 + h])
        fz_own[h].start()
        fz_sib.append(push(own, Fz[h].at[z, c], gsnd.at[h, 0], grcv.at[h, 0], sibling))

    def feature_forward(h):
        for dz in (1, 3, 2):
            fz_copies[h, dz].wait_recv()
            zs = lax.rem(z - dz + 4, 4)
            fz_sib.append(push(Fz[h].at[zs, c], Fz[h].at[zs, c], gsnd.at[h, dz], grcv.at[h, dz], sibling))

    matmul_head(0, F, W1o, W1s, Ao, As)
    matmul_tail(0, F, W1o, W1s, Ao, As, asnd, arcv)
    acc0 = push(As0, Ar0, dsnd.at[0], drcv.at[0], sibling)
    feature_exchange(0)
    matmul_head(1, F, W1o, W1s, Ao, As)
    acc0.wait_recv()
    H0[me] = jnp.tanh(Ao0[...] + Ar0[...]).astype(BF16)
    first0 = gather_send(0, H, bsnd, brcv)
    matmul_tail(1, F, W1o, W1s, Ao, As, asnd, arcv)
    acc1 = push(As1, Ar1, dsnd.at[1], drcv.at[1], sibling)
    feature_exchange(1)
    gather_forward(0, H, bsnd, brcv, first0)
    acc1.wait_recv()
    H1[me] = jnp.tanh(Ao1[...] + Ar1[...]).astype(BF16)
    first1 = gather_send(1, H, bsnd, brcv)
    w2_own.wait()
    w2_sib.wait_recv()

    weights = head[...]
    back_copies, coef_copies = {}, {}

    def head_terms(h):
        act = jnp.tanh(Bo[h][...] + Br[h][...])
        Co[h][...] = (weights * (1.0 - act * act)).astype(BF16)
        coef_copies[h] = push(Co[h], Cs[h], dsnd.at[4 + h], drcv.at[4 + h], sibling)
        part = jnp.sum(act * weights, axis=1, keepdims=True)
        SC[h : h + 1] = to_row(part[0:NP])
        if h == 0:
            queries = jnp.concatenate([part[NP:144], jnp.zeros((128 - NQ, 1), F32)], axis=0)
            SC[2:3] = to_row(queries)

    def back_block(h, k):
        return dot_nt(Co[h][...], W2o[k]) + dot_nt(Cs[h][...], W2s[k])

    order = (2, 1, 3, 0)

    def back_send(h):
        coef_copies[h].wait_recv()
        for da in order:
            for e in (2, 1, 3):
                k = plane(da, e)
                Pb[h][k] = back_block(h, k).astype(BF16)
                i = 3 * da + e - 1
                back_copies[h, da, e] = push(
                    Pb[h].at[k], RB[h].at[i], csnd.at[h, i], crcv.at[h, i], dev(0, e)
                )

    def back_own(h):
        for da in order:
            Sa[h][da] = back_block(h, plane(da, 0))

    def back_sum(h):
        for da in order:
            total = Sa[h][da]
            for e in (1, 3, 2):
                back_copies[h, da, e].wait_recv()
                total += RB[h][3 * da + e - 1].astype(F32)
            if da:
                k = plane(da, 0)
                Pb[h][k] = total.astype(BF16)
                back_copies[h, da, 0] = push(
                    Pb[h].at[k], RA[h].at[da - 1], csnd.at[h, 11 + da], crcv.at[h, 11 + da], dev(da, 0)
                )
            else:
                Sa[h][0] = total

    def mixing_of(h):
        total = Sa[h][0]
        for d in (1, 3, 2):
            back_copies[h, d, 0].wait_recv()
            total += RA[h][d - 1].astype(F32)
        own = H[h][me].astype(F32)
        return (1.0 - own * own) * total

    SC[...] = jnp.zeros((8, 128), F32)
    matmul_head(0, H, W2o, W2s, Bo, Bs)
    gather_forward(1, H, bsnd, brcv, first1)
    matmul_tail(0, H, W2o, W2s, Bo, Bs, bsnd, brcv)
    acc0 = push(Bs0, Br0, dsnd.at[2], drcv.at[2], sibling)
    matmul_head(1, H, W2o, W2s, Bo, Bs)
    acc0.wait_recv()
    head_terms(0)
    back_send(0)
    matmul_tail(1, H, W2o, W2s, Bo, Bs, bsnd, brcv)
    acc1 = push(Bs1, Br1, dsnd.at[3], drcv.at[3], sibling)
    back_own(0)
    acc1.wait_recv()
    head_terms(1)
    pair = push(SC, SCr, dsnd.at[6], drcv.at[6], sibling)
    back_send(1)
    pair.wait_recv()
    SP[...] = SC[...] + SCr[...]
    scores = [
        push(SP, SPr.at[i], ssnd.at[i], srcv.at[i], dev(da, db)) for i, (da, db) in enumerate(offsets)
    ]
    feature_forward(0)
    back_sum(0)
    back_own(1)
    feature_forward(1)

    score = SP[...]
    for i, copy in enumerate(scores):
        copy.wait_recv()
        score += SPr[i]
    SZ[0] = score
    sz = [push(SZ.at[0], SZ.at[d], ssnd.at[14 + d], srcv.at[14 + d], zdev(d)) for d in (1, 2, 3)]

    mixing = mixing_of(0)
    margin = score[2:3] - pltpu.roll(score[2:3], 120, 1)
    signed = 2.0 * qclicks[...].astype(F32) - 1.0
    slope_query = -signed * jax.nn.sigmoid(-signed * margin[:, 0:8])
    err_row = jnp.concatenate([slope_query, -slope_query, jnp.zeros((1, 112), F32)], axis=1)
    err = to_column(err_row)[0:NQ]
    QA[z] = (err * mixing[NP:144]).astype(BF16)
    qa = [push(QA.at[z], QA.at[z], msnd.at[d - 1], mrcv.at[d - 1], zdev(d)) for d in (1, 2, 3)]
    MX[0, z] = mixing[0:NP].astype(BF16)
    mx = [push(MX.at[0, z], MX.at[0, z], msnd.at[2 + d], mrcv.at[2 + d], zdev(d)) for d in (1, 2, 3)]

    back_sum(1)
    fz_own[0].wait()
    fz_own[1].wait()
    for copy in fz_sib:
        copy.wait_recv()

    @pl.loop(0, 8)
    def _(b):
        par, k = lax.rem(b, 2), lax.div(b, 2)
        queries = jnp.concatenate([Fz0[zz, par, k, NP:144] for zz in range(4)], axis=0)
        FU[b] = queries.astype(F32).T.astype(BF16)

    kt = []
    for dz in (2, 1, 3, 0):
        zt = lax.rem(z + dz, 4)
        for h in range(2):
            total = jnp.zeros((NP, 4 * NQ), F32)
            for b in range(8):
                total += dot(Fz[h][zt, b % 2, b // 2, 0:NP], FU[b])
            KT[4 + dz, h] = total
        if dz:
            kt.append(push(KT.at[4 + dz], KT.at[dz], ksnd.at[dz - 1], krcv.at[dz - 1], zdev(dz)))

    for copy in qa:
        copy.wait_recv()
    squares = jnp.zeros((1, W), F32)
    query_rows = jnp.concatenate([QA[zz] for zz in range(4)], axis=0)
    for b in range(8):
        block = dot(FU[b], query_rows)
        squares += jnp.sum(block * block, axis=0, keepdims=True)
        Gf[b] = block
    g_copy = pltpu.make_async_copy(Gf, g_out, loc.at[4])
    g_copy.start()
    norm_part = jnp.broadcast_to(jnp.sum(squares, axis=1, keepdims=True), (8, 128))
    cross_rows = KT[4]
    for copy in kt:
        copy.wait_recv()
    for dz in (1, 2, 3):
        cross_rows += KT[dz]
    cross_rows = cross_rows.astype(BF16)

    second = mixing_of(1)
    MX[1, z] = second.astype(BF16)
    mx += [push(MX.at[1, z], MX.at[1, z], msnd.at[5 + d], mrcv.at[5 + d], zdev(d)) for d in (1, 2, 3)]
    own_response = []
    for h, rows in enumerate((mixing[0:NP], second)):
        project = dot(cross_rows[h], query_rows)
        own_response.append(to_row(jnp.sum(rows * project, axis=1, keepdims=True)))
    replica = lax.broadcasted_iota(jnp.int32, (4, 128), 0) == z
    own_tile = jnp.concatenate(
        [jnp.where(replica, jnp.broadcast_to(row, (4, 128)), 0.0) for row in own_response], axis=0
    )

    def all_reduce(tile, turn, between):
        base = turn * 19
        AR[turn] = tile
        pair = push(AR.at[turn], ARr.at[turn], rsnd.at[base], rrcv.at[base], sibling)
        pair.wait_recv()
        tile = AR[turn] + ARr[turn]
        ARp[turn] = tile
        copies = [
            push(ARp.at[turn], ARpr.at[turn, i], rsnd.at[base + 1 + i], rrcv.at[base + 1 + i], dev(da, db))
            for i, (da, db) in enumerate(offsets)
        ]
        between()
        for i, copy in enumerate(copies):
            copy.wait_recv()
            tile += ARpr[turn, i]
        ARz[turn, 0] = tile
        copies = [
            push(ARz.at[turn, 0], ARz.at[turn, d], rsnd.at[base + 15 + d], rrcv.at[base + 15 + d], zdev(d))
            for d in (1, 2, 3)
        ]
        for d, copy in enumerate(copies):
            copy.wait_recv()
            tile += ARz[turn, d + 1]
        return tile

    def transposes():
        @pl.loop(0, 8)
        def _(b):
            par, k = lax.rem(b, 2), lax.div(b, 2)
            for h in range(2):
                for zz in range(4):
                    at = (4 * h + zz) * NP
                    FT[b, :, at : at + NP] = Fz[h][zz, par, k, 0:NP].T

    tile = all_reduce(jnp.concatenate([own_tile, norm_part], axis=0), 0, transposes)

    for copy in sz:
        copy.wait_recv()
    train_margin = []
    for zz in range(4):
        other = SZ[lax.rem(z - zz + 4, 4)]
        train_margin.append(other[0:1] - other[1:2])
    margins = jnp.concatenate(train_margin, axis=0)
    curve = jax.nn.sigmoid(margins) * jax.nn.sigmoid(-margins)
    for copy in mx:
        copy.wait_recv()

    rdiff_first = tile[0:4] - tile[4:8]
    norm_first = tile[8:9, 0:1]
    resp_err = curve * rdiff_first
    for zz in range(4):
        scale = to_column(resp_err[zz : zz + 1])
        R0[zz * NP : (zz + 1) * NP] = (scale * MX[0, zz].astype(F32)).astype(BF16)
        R0[(4 + zz) * NP : (5 + zz) * NP] = (-scale * MX[1, zz].astype(F32)).astype(BF16)
    for b in range(8):
        block = dot(FT[b], R0[...])
        Pf[b] = block
        Pp[b] = block.astype(BF16)
    p_copy = pltpu.make_async_copy(Pf, p_out, loc.at[5])
    p_copy.start()

    response = []
    for h in range(2):
        for zz in range(4):
            project = jnp.zeros((NP, W), F32)
            for b in range(8):
                project += dot(Fz[h][zz, b % 2, b // 2, 0:NP], Pp[b])
            response.append(to_row(jnp.sum(MX[h, zz].astype(F32) * project, axis=1, keepdims=True)))
    tile = all_reduce(jnp.concatenate(response + [norm_part], axis=0), 1, lambda: None)
    rdiff_prod = tile[0:4] - tile[4:8]

    def total_of(value):
        return jnp.sum(jnp.sum(value, axis=1, keepdims=True), axis=0, keepdims=True)

    cross = total_of(curve * rdiff_first * rdiff_first)
    prod_norm = total_of(curve * rdiff_first * rdiff_prod)
    curv_first = cross + DAMPING * norm_first
    alpha_first = norm_first / curv_first
    keep = 1.0 - DAMPING * alpha_first
    norm_next = keep * keep * norm_first - 2.0 * keep * alpha_first * cross + alpha_first * alpha_first * prod_norm
    lead = keep + norm_next / norm_first
    rdiff_next = lead * rdiff_first - alpha_first * rdiff_prod
    direction_norm = lead * lead * norm_first - 2.0 * lead * alpha_first * cross + alpha_first * alpha_first * prod_norm
    curv_next = total_of(curve * rdiff_next * rdiff_next) + DAMPING * direction_norm
    alpha_next = norm_next / curv_next
    on_gradient = alpha_first + alpha_next * lead
    on_product = -alpha_next * alpha_first

    own_margin = score[0:1] - score[1:2]
    signed = 2.0 * clicks[...].astype(F32) - 1.0
    slope = -signed * jax.nn.sigmoid(-signed * own_margin)
    change = alpha_first * rdiff_first + alpha_next * rdiff_next
    on_g[...] = jnp.broadcast_to(on_gradient, (1, W))
    on_p[...] = jnp.broadcast_to(on_product, (1, W))
    infl[...] = -slope * jnp.sum(jnp.where(replica, change, 0.0), axis=0, keepdims=True)

    g_copy.wait()
    p_copy.wait()
    for copy in sent:
        copy.wait_send()


def local(logged, pairs, clicks, query_pairs, query_clicks, first_weight, second_weight, head_weight):
    vmem = pl.BlockSpec(memory_space=pltpu.VMEM)
    hbm = pl.BlockSpec(memory_space=pl.ANY)
    V = pltpu.VMEM
    dma = pltpu.SemaphoreType.DMA

    def halves(dtype, *lead):
        return [V((*lead, rows, W), dtype) for rows in HALF]

    scratch = (
        halves(BF16, 16) + halves(BF16, 16)
        + [V((16, W, W), BF16)] * 4
        + halves(F32) * 6
        + halves(BF16) * 2
        + halves(BF16, 16) + halves(BF16, 12) + halves(F32, 4) + halves(BF16, 3)
        + halves(BF16, 4, 2, 4)
        + [V((8, W, 8 * NP), BF16), V((8, W, 4 * NQ), BF16)]
        + [V((8, 2, NP, 4 * NQ), F32)]
        + [V((2, 4, NP, W), BF16), V((4, NQ, W), BF16)]
        + [V((8, 128), F32)] * 3 + [V((15, 8, 128), F32), V((4, 8, 128), F32)]
        + [V((8, W, W), F32), V((8, W, W), F32), V((8, W, W), BF16)]
        + [V((8 * NP, W), BF16)]
        + [V((2, 16, 128), F32)] * 3 + [V((2, 15, 16, 128), F32), V((2, 4, 16, 128), F32)]
        + [dma((6,))]
        + [dma((2,))] * 2 + [dma((2, 15))] * 6 + [dma((7,))] * 2
        + [dma((2, 3))] * 2 + [dma((2, 4))] * 2 + [dma((3,))] * 2
        + [dma((9,))] * 2 + [dma((18,))] * 2 + [dma((38,))] * 2
    )
    gradient, product, on_gradient, on_product, influence = pl.pallas_call(
        kernel,
        out_shape=(
            jax.ShapeDtypeStruct((8, W, W), F32),
            jax.ShapeDtypeStruct((8, W, W), F32),
            jax.ShapeDtypeStruct((1, W), F32),
            jax.ShapeDtypeStruct((1, W), F32),
            jax.ShapeDtypeStruct((1, NP), F32),
        ),
        in_specs=[vmem, vmem, vmem, vmem, vmem, hbm, hbm, vmem],
        out_specs=(hbm, hbm, vmem, vmem, vmem),
        scratch_shapes=scratch,
        compiler_params=pltpu.CompilerParams(
            collective_id=0, has_side_effects=True, vmem_limit_bytes=60 << 20
        ),
    )(
        logged,
        pairs.T,
        clicks.reshape(1, NP),
        query_pairs.T,
        query_clicks.reshape(1, 8),
        first_weight.reshape(16, 2, W, W),
        second_weight.reshape(16, 2, W, W),
        head_weight.reshape(1, W),
    )
    solved = on_gradient * gradient.reshape(8 * W, W) + on_product * product.reshape(8 * W, W)
    return (solved, influence.reshape(NP))


def solution(mesh):
    placed = (
        P("dp", "fsdp"),
        P("dp", None),
        P("dp"),
        P("dp", None),
        P("dp"),
        P(None, "fsdp"),
        P(None, "fsdp"),
        P("fsdp"),
    )
    return jax.shard_map(
        local, mesh=mesh, in_specs=placed, out_specs=(P("dp", "fsdp"), P("dp")), check_vma=False
    )
```

```python
import jax
import jax.numpy as jnp
from jax import lax
from jax.experimental import pallas as pl
from jax.experimental.pallas import tpu as pltpu
from jax.sharding import PartitionSpec as P

DAMPING = 0.01
MESH = pl.DeviceIdType.MESH
F32 = jnp.float32
BF16 = jnp.bfloat16

NP = 128
NQ = 16
HALF = (144, 128)
W = 256
SPLIT_A = 6
SPLIT_B = 6


def dot(left, right):
    return jnp.dot(left, right, preferred_element_type=F32)


def dot_nt(left, right):
    return lax.dot_general(left, right, (((1,), (1,)), ((), ())), preferred_element_type=F32)


def kernel(
    logged, pairs, clicks, qpairs, qclicks, w1, w2, head,
    g_out, p_out, on_g, on_p, infl,
    F0, F1, H0, H1, W1o, W1s, W2o, W2s,
    Ao0, Ao1, As0, As1, Ar0, Ar1, Bo0, Bo1, Bs0, Bs1, Br0, Br1,
    Co0, Co1, Cs0, Cs1, Pb0, Pb1, RB0, RB1, Sa0, Sa1, RA0, RA1,
    Fz0, Fz1, FT, FU, KT, MX, QA, SC, SCr, SP, SPr, SZ, Gp, Pp, R0,
    AR, ARr, ARp, ARpr, ARz,
    loc, wsnd, wrcv, asnd, arcv, bsnd, brcv, csnd, crcv, dsnd, drcv, fsnd, frcv, gsnd, grcv,
    ksnd, krcv, msnd, mrcv, ssnd, srcv, rsnd, rrcv,
):
    F, H = (F0, F1), (H0, H1)
    Ao, As, Ar = (Ao0, Ao1), (As0, As1), (Ar0, Ar1)
    Bo, Bs, Br = (Bo0, Bo1), (Bs0, Bs1), (Br0, Br1)
    Co, Cs = (Co0, Co1), (Cs0, Cs1)
    Pb, RB, Sa, RA = (Pb0, Pb1), (RB0, RB1), (Sa0, Sa1), (RA0, RA1)
    Fz = (Fz0, Fz1)

    z = lax.axis_index("dp")
    f = lax.axis_index("fsdp")
    c = lax.rem(f, 2)
    me = lax.div(f, 2)
    x = lax.rem(me, 4)
    y = lax.div(me, 4)

    def plane(da, db):
        nx = lax.rem(x + da * (1 - c) + db * c + 8, 4)
        ny = lax.rem(y + da * c + db * (1 - c) + 8, 4)
        return ny * 4 + nx

    def dev(da, db):
        return (z, plane(da, db) * 2 + c)

    def zdev(dz):
        return (lax.rem(z + dz + 4, 4), f)

    sibling = (z, me * 2 + 1 - c)
    offsets = [(da, db) for da in range(4) for db in range(4) if (da, db) != (0, 0)]
    partners = [sibling] + [dev(da, db) for da, db in offsets] + [zdev(d) for d in (1, 2, 3)]
    barrier = pltpu.get_barrier_semaphore()
    for partner in partners:
        pl.semaphore_signal(barrier, inc=1, device_id=partner, device_id_type=MESH)
    pl.semaphore_wait(barrier, len(partners))

    sent = []

    def remote(src, dst, send_sem, recv_sem, device):
        return pltpu.make_async_remote_copy(
            src_ref=src, dst_ref=dst, send_sem=send_sem, recv_sem=recv_sem,
            device_id=device, device_id_type=MESH,
        )

    def push(src, dst, send_sem, recv_sem, device):
        copy = remote(src, dst, send_sem, recv_sem, device)
        copy.start()
        sent.append(copy)
        return copy

    rows128 = lax.broadcasted_iota(jnp.int32, (128, 128), 0)
    lanes128 = lax.broadcasted_iota(jnp.int32, (128, 128), 1)
    eye = rows128 == lanes128

    def to_row(column):
        return jnp.sum(jnp.where(eye, jnp.broadcast_to(column, (128, 128)), 0.0), axis=0, keepdims=True)

    def to_column(row):
        return jnp.sum(jnp.where(eye, jnp.broadcast_to(row, (128, 128)), 0.0), axis=1, keepdims=True)

    w1_own = pltpu.make_async_copy(w1.at[:, c], W1o, loc.at[0])
    w2_own = pltpu.make_async_copy(w2.at[:, c], W2o, loc.at[1])
    w1_own.start()
    w1_sib = push(w1.at[:, 1 - c], W1s, wsnd.at[0], wrcv.at[0], sibling)

    def gather_send(h, buf, snd, rcv):
        first = {}
        for d in (2, 1, 3):
            first[d] = push(buf[h].at[me], buf[h].at[me], snd.at[h, d - 1], rcv.at[h, d - 1], dev(d, 0))
        return first

    def gather_across(h, buf, snd, rcv):
        for e in (2, 1, 3):
            push(buf[h].at[me], buf[h].at[me], snd.at[h, 2 + e], rcv.at[h, 2 + e], dev(0, e))

    def gather_forward(h, buf, snd, rcv, first):
        for d in (1, 3, 2):
            first[d].wait_recv()
            slot = plane(-d, 0)
            for e in (2, 1, 3):
                i = 3 * d + 2 + e
                push(buf[h].at[slot], buf[h].at[slot], snd.at[h, i], rcv.at[h, i], dev(0, e))

    def matmul_head(h, buf, wo, ws, acc_o, acc_s):
        block = buf[h][me]
        acc_o[h][...] = dot(block, wo[me])
        acc_s[h][...] = dot(block, ws[me])

        @pl.loop(1, 4)
        def _(d):
            slot = plane(-d, 0)
            block = buf[h][slot]
            acc_o[h][...] += dot(block, wo[slot])
            acc_s[h][...] += dot(block, ws[slot])

    def matmul_tail(h, buf, wo, ws, acc_o, acc_s, snd, rcv, start, stop):
        @pl.loop(start, stop)
        def _(i):
            slot = plane(-lax.div(i, 3), -(lax.rem(i, 3) + 1))
            remote(buf[h].at[slot], buf[h].at[slot], snd.at[h, 3 + i], rcv.at[h, 3 + i], sibling).wait_recv()
            block = buf[h][slot]
            acc_o[h][...] += dot(block, wo[slot])
            acc_s[h][...] += dot(block, ws[slot])

    def select(row, count):
        lanes = lax.broadcasted_iota(jnp.int32, (128, 512), 1)
        ids = to_column(row.astype(F32)).astype(jnp.int32)
        return dot((ids == lanes).astype(F32).astype(BF16)[0:count], logged[...]).astype(BF16)

    F0[me, 0:NP] = select(pairs[0:1], NP)
    query_ids = jnp.concatenate([qpairs[0:1], qpairs[1:2], jnp.zeros((1, 112), jnp.int32)], axis=1)
    F0[me, NP:144] = select(query_ids, NQ)
    first0 = gather_send(0, F, asnd, arcv)
    gather_across(0, F, asnd, arcv)
    F1[me] = select(pairs[1:2], NP)
    first1 = gather_send(1, F, asnd, arcv)
    gather_forward(0, F, asnd, arcv, first0)
    w1_own.wait()
    w1_sib.wait_recv()
    w2_own.start()
    w2_sib = push(w2.at[:, 1 - c], W2s, wsnd.at[1], wrcv.at[1], sibling)

    fz_copies, fz_own, fz_sib = {}, {}, []

    def feature_exchange(h):
        for dz in (1, 3, 2):
            z2 = lax.rem(z + dz, 4)
            fz_copies[h, dz] = push(
                F[h].at[pl.ds(4 * z2, 4)], Fz[h].at[z, c], fsnd.at[h, dz - 1], frcv.at[h, dz - 1], zdev(dz)
            )
        own = F[h].at[pl.ds(4 * z, 4)]
        fz_own[h] = pltpu.make_async_copy(own, Fz[h].at[z, c], loc.at[2 + h])
        fz_own[h].start()
        fz_sib.append(push(own, Fz[h].at[z, c], gsnd.at[h, 0], grcv.at[h, 0], sibling))

    def feature_forward(h):
        for dz in (1, 3, 2):
            fz_copies[h, dz].wait_recv()
            zs = lax.rem(z - dz + 4, 4)
            fz_sib.append(push(Fz[h].at[zs, c], Fz[h].at[zs, c], gsnd.at[h, dz], grcv.at[h, dz], sibling))

    matmul_head(0, F, W1o, W1s, Ao, As)
    matmul_tail(0, F, W1o, W1s, Ao, As, asnd, arcv, 0, SPLIT_A)
    gather_across(1, F, asnd, arcv)
    gather_forward(1, F, asnd, arcv, first1)
    matmul_tail(0, F, W1o, W1s, Ao, As, asnd, arcv, SPLIT_A, 12)
    acc0 = push(As0, Ar0, dsnd.at[0], drcv.at[0], sibling)
    feature_exchange(0)
    matmul_head(1, F, W1o, W1s, Ao, As)
    acc0.wait_recv()
    H0[me] = jnp.tanh(Ao0[...] + Ar0[...]).astype(BF16)
    first0 = gather_send(0, H, bsnd, brcv)
    gather_across(0, H, bsnd, brcv)
    matmul_tail(1, F, W1o, W1s, Ao, As, asnd, arcv, 0, SPLIT_B)
    gather_forward(0, H, bsnd, brcv, first0)
    matmul_tail(1, F, W1o, W1s, Ao, As, asnd, arcv, SPLIT_B, 12)
    acc1 = push(As1, Ar1, dsnd.at[1], drcv.at[1], sibling)
    feature_exchange(1)
    acc1.wait_recv()
    H1[me] = jnp.tanh(Ao1[...] + Ar1[...]).astype(BF16)
    first1 = gather_send(1, H, bsnd, brcv)
    w2_own.wait()
    w2_sib.wait_recv()

    weights = head[...]
    back_copies, coef_copies = {}, {}

    def head_terms(h):
        act = jnp.tanh(Bo[h][...] + Br[h][...])
        Co[h][...] = (weights * (1.0 - act * act)).astype(BF16)
        coef_copies[h] = push(Co[h], Cs[h], dsnd.at[4 + h], drcv.at[4 + h], sibling)
        part = jnp.sum(act * weights, axis=1, keepdims=True)
        SC[h : h + 1] = to_row(part[0:NP])
        if h == 0:
            queries = jnp.concatenate([part[NP:144], jnp.zeros((128 - NQ, 1), F32)], axis=0)
            SC[2:3] = to_row(queries)

    def back_block(h, k):
        return dot_nt(Co[h][...], W2o[k]) + dot_nt(Cs[h][...], W2s[k])

    order = (2, 1, 3, 0)

    def back_send(h):
        coef_copies[h].wait_recv()
        for da in order:
            for e in (2, 1, 3):
                k = plane(da, e)
                Pb[h][k] = back_block(h, k).astype(BF16)
                i = 3 * da + e - 1
                back_copies[h, da, e] = push(
                    Pb[h].at[k], RB[h].at[i], csnd.at[h, i], crcv.at[h, i], dev(0, e)
                )

    def back_own(h):
        for da in order:
            Sa[h][da] = back_block(h, plane(da, 0))

    def back_sum(h):
        for da in order:
            total = Sa[h][da]
            for e in (1, 3, 2):
                back_copies[h, da, e].wait_recv()
                total += RB[h][3 * da + e - 1].astype(F32)
            if da:
                k = plane(da, 0)
                Pb[h][k] = total.astype(BF16)
                back_copies[h, da, 0] = push(
                    Pb[h].at[k], RA[h].at[da - 1], csnd.at[h, 11 + da], crcv.at[h, 11 + da], dev(da, 0)
                )
            else:
                Sa[h][0] = total

    def mixing_of(h):
        total = Sa[h][0]
        for d in (1, 3, 2):
            back_copies[h, d, 0].wait_recv()
            total += RA[h][d - 1].astype(F32)
        own = H[h][me].astype(F32)
        return (1.0 - own * own) * total

    SC[...] = jnp.zeros((8, 128), F32)
    matmul_head(0, H, W2o, W2s, Bo, Bs)
    matmul_tail(0, H, W2o, W2s, Bo, Bs, bsnd, brcv, 0, SPLIT_A)
    gather_across(1, H, bsnd, brcv)
    gather_forward(1, H, bsnd, brcv, first1)
    matmul_tail(0, H, W2o, W2s, Bo, Bs, bsnd, brcv, SPLIT_A, 12)
    acc0 = push(Bs0, Br0, dsnd.at[2], drcv.at[2], sibling)
    matmul_head(1, H, W2o, W2s, Bo, Bs)
    acc0.wait_recv()
    head_terms(0)
    back_send(0)
    matmul_tail(1, H, W2o, W2s, Bo, Bs, bsnd, brcv, 0, 12)
    acc1 = push(Bs1, Br1, dsnd.at[3], drcv.at[3], sibling)
    back_own(0)
    acc1.wait_recv()
    head_terms(1)
    pair = push(SC, SCr, dsnd.at[6], drcv.at[6], sibling)
    back_send(1)
    pair.wait_recv()
    SP[...] = SC[...] + SCr[...]
    scores = [
        push(SP, SPr.at[i], ssnd.at[i], srcv.at[i], dev(da, db)) for i, (da, db) in enumerate(offsets)
    ]
    feature_forward(0)
    back_own(1)
    feature_forward(1)
    back_sum(0)
    fz_own[0].wait()
    fz_own[1].wait()
    for copy in fz_sib:
        copy.wait_recv()

    @pl.loop(0, 8)
    def _(b):
        par, k = lax.rem(b, 2), lax.div(b, 2)
        queries = jnp.concatenate([Fz0[zz, par, k, NP:144] for zz in range(4)], axis=0)
        FU[b] = queries.astype(F32).T.astype(BF16)

    kt = []
    for dz in (2, 1, 3, 0):
        zt = lax.rem(z + dz, 4)
        for h in range(2):
            total = jnp.zeros((NP, 4 * NQ), F32)
            for b in range(8):
                total += dot(Fz[h][zt, b % 2, b // 2, 0:NP], FU[b])
            KT[4 + dz, h] = total
        if dz:
            kt.append(push(KT.at[4 + dz], KT.at[dz], ksnd.at[dz - 1], krcv.at[dz - 1], zdev(dz)))

    score = SP[...]
    for i, copy in enumerate(scores):
        copy.wait_recv()
        score += SPr[i]
    SZ[0] = score
    sz = [push(SZ.at[0], SZ.at[d], ssnd.at[14 + d], srcv.at[14 + d], zdev(d)) for d in (1, 2, 3)]

    mixing = mixing_of(0)
    margin = score[2:3] - pltpu.roll(score[2:3], 120, 1)
    signed = 2.0 * qclicks[...].astype(F32) - 1.0
    slope_query = -signed * jax.nn.sigmoid(-signed * margin[:, 0:8])
    err_row = jnp.concatenate([slope_query, -slope_query, jnp.zeros((1, 112), F32)], axis=1)
    err = to_column(err_row)[0:NQ]
    QA[z] = (err * mixing[NP:144]).astype(BF16)
    qa = [push(QA.at[z], QA.at[z], msnd.at[d - 1], mrcv.at[d - 1], zdev(d)) for d in (1, 2, 3)]
    MX[0, z] = mixing[0:NP].astype(BF16)
    mx = [push(MX.at[0, z], MX.at[0, z], msnd.at[2 + d], mrcv.at[2 + d], zdev(d)) for d in (1, 2, 3)]

    back_sum(1)
    for copy in qa:
        copy.wait_recv()
    squares = jnp.zeros((1, W), F32)
    query_rows = jnp.concatenate([QA[zz] for zz in range(4)], axis=0)
    for b in range(8):
        block = dot(FU[b], query_rows)
        squares += jnp.sum(block * block, axis=0, keepdims=True)
        Gp[b] = block.astype(BF16)
    g_copy = pltpu.make_async_copy(Gp, g_out, loc.at[4])
    g_copy.start()
    norm_part = jnp.broadcast_to(jnp.sum(squares, axis=1, keepdims=True), (8, 128))
    cross_rows = KT[4]
    for copy in kt:
        copy.wait_recv()
    for dz in (1, 2, 3):
        cross_rows += KT[dz]
    cross_rows = cross_rows.astype(BF16)

    second = mixing_of(1)
    MX[1, z] = second.astype(BF16)
    mx += [push(MX.at[1, z], MX.at[1, z], msnd.at[5 + d], mrcv.at[5 + d], zdev(d)) for d in (1, 2, 3)]
    own_response = []
    for h, rows in enumerate((mixing[0:NP], second)):
        project = dot(cross_rows[h], query_rows)
        own_response.append(to_row(jnp.sum(rows * project, axis=1, keepdims=True)))
    replica = lax.broadcasted_iota(jnp.int32, (4, 128), 0) == z
    own_tile = jnp.concatenate(
        [jnp.where(replica, jnp.broadcast_to(row, (4, 128)), 0.0) for row in own_response], axis=0
    )

    def all_reduce(tile, turn, between):
        base = turn * 19
        AR[turn] = tile
        pair = push(AR.at[turn], ARr.at[turn], rsnd.at[base], rrcv.at[base], sibling)
        pair.wait_recv()
        tile = AR[turn] + ARr[turn]
        ARp[turn] = tile
        copies = [
            push(ARp.at[turn], ARpr.at[turn, i], rsnd.at[base + 1 + i], rrcv.at[base + 1 + i], dev(da, db))
            for i, (da, db) in enumerate(offsets)
        ]
        between()
        for i, copy in enumerate(copies):
            copy.wait_recv()
            tile += ARpr[turn, i]
        ARz[turn, 0] = tile
        copies = [
            push(ARz.at[turn, 0], ARz.at[turn, d], rsnd.at[base + 15 + d], rrcv.at[base + 15 + d], zdev(d))
            for d in (1, 2, 3)
        ]
        for d, copy in enumerate(copies):
            copy.wait_recv()
            tile += ARz[turn, d + 1]
        return tile

    def transposes():
        @pl.loop(0, 8)
        def _(b):
            par, k = lax.rem(b, 2), lax.div(b, 2)
            for h in range(2):
                for zz in range(4):
                    at = (4 * h + zz) * NP
                    FT[b, :, at : at + NP] = Fz[h][zz, par, k, 0:NP].T

    tile = all_reduce(jnp.concatenate([own_tile, norm_part], axis=0), 0, transposes)

    for copy in sz:
        copy.wait_recv()
    train_margin = []
    for zz in range(4):
        other = SZ[lax.rem(z - zz + 4, 4)]
        train_margin.append(other[0:1] - other[1:2])
    margins = jnp.concatenate(train_margin, axis=0)
    curve = jax.nn.sigmoid(margins) * jax.nn.sigmoid(-margins)
    for copy in mx:
        copy.wait_recv()

    rdiff_first = tile[0:4] - tile[4:8]
    norm_first = tile[8:9, 0:1]
    resp_err = curve * rdiff_first
    for zz in range(4):
        scale = to_column(resp_err[zz : zz + 1])
        R0[zz * NP : (zz + 1) * NP] = (scale * MX[0, zz].astype(F32)).astype(BF16)
        R0[(4 + zz) * NP : (5 + zz) * NP] = (-scale * MX[1, zz].astype(F32)).astype(BF16)
    for b in range(8):
        block = dot(FT[b], R0[...])
        Pp[b] = block.astype(BF16)
    p_copy = pltpu.make_async_copy(Pp, p_out, loc.at[5])
    p_copy.start()

    response = []
    for h in range(2):
        for zz in range(4):
            project = jnp.zeros((NP, W), F32)
            for b in range(8):
                project += dot(Fz[h][zz, b % 2, b // 2, 0:NP], Pp[b])
            response.append(to_row(jnp.sum(MX[h, zz].astype(F32) * project, axis=1, keepdims=True)))
    tile = all_reduce(jnp.concatenate(response + [norm_part], axis=0), 1, lambda: None)
    rdiff_prod = tile[0:4] - tile[4:8]

    def total_of(value):
        return jnp.sum(jnp.sum(value, axis=1, keepdims=True), axis=0, keepdims=True)

    cross = total_of(curve * rdiff_first * rdiff_first)
    prod_norm = total_of(curve * rdiff_first * rdiff_prod)
    curv_first = cross + DAMPING * norm_first
    alpha_first = norm_first / curv_first
    keep = 1.0 - DAMPING * alpha_first
    norm_next = keep * keep * norm_first - 2.0 * keep * alpha_first * cross + alpha_first * alpha_first * prod_norm
    lead = keep + norm_next / norm_first
    rdiff_next = lead * rdiff_first - alpha_first * rdiff_prod
    direction_norm = lead * lead * norm_first - 2.0 * lead * alpha_first * cross + alpha_first * alpha_first * prod_norm
    curv_next = total_of(curve * rdiff_next * rdiff_next) + DAMPING * direction_norm
    alpha_next = norm_next / curv_next
    on_gradient = alpha_first + alpha_next * lead
    on_product = -alpha_next * alpha_first

    own_margin = score[0:1] - score[1:2]
    signed = 2.0 * clicks[...].astype(F32) - 1.0
    slope = -signed * jax.nn.sigmoid(-signed * own_margin)
    change = alpha_first * rdiff_first + alpha_next * rdiff_next
    on_g[...] = jnp.broadcast_to(on_gradient, (1, W))
    on_p[...] = jnp.broadcast_to(on_product, (1, W))
    infl[...] = -slope * jnp.sum(jnp.where(replica, change, 0.0), axis=0, keepdims=True)

    g_copy.wait()
    p_copy.wait()
    for copy in sent:
        copy.wait_send()


def local(logged, pairs, clicks, query_pairs, query_clicks, first_weight, second_weight, head_weight):
    vmem = pl.BlockSpec(memory_space=pltpu.VMEM)
    hbm = pl.BlockSpec(memory_space=pl.ANY)
    V = pltpu.VMEM
    dma = pltpu.SemaphoreType.DMA

    def halves(dtype, *lead):
        return [V((*lead, rows, W), dtype) for rows in HALF]

    scratch = (
        halves(BF16, 16) + halves(BF16, 16)
        + [V((16, W, W), BF16)] * 4
        + halves(F32) * 6
        + halves(BF16) * 2
        + halves(BF16, 16) + halves(BF16, 12) + halves(F32, 4) + halves(BF16, 3)
        + halves(BF16, 4, 2, 4)
        + [V((8, W, 8 * NP), BF16), V((8, W, 4 * NQ), BF16)]
        + [V((8, 2, NP, 4 * NQ), F32)]
        + [V((2, 4, NP, W), BF16), V((4, NQ, W), BF16)]
        + [V((8, 128), F32)] * 3 + [V((15, 8, 128), F32), V((4, 8, 128), F32)]
        + [V((8, W, W), BF16)] * 2
        + [V((8 * NP, W), BF16)]
        + [V((2, 16, 128), F32)] * 3 + [V((2, 15, 16, 128), F32), V((2, 4, 16, 128), F32)]
        + [dma((6,))]
        + [dma((2,))] * 2 + [dma((2, 15))] * 6 + [dma((7,))] * 2
        + [dma((2, 3))] * 2 + [dma((2, 4))] * 2 + [dma((3,))] * 2
        + [dma((9,))] * 2 + [dma((18,))] * 2 + [dma((38,))] * 2
    )
    gradient, product, on_gradient, on_product, influence = pl.pallas_call(
        kernel,
        out_shape=(
            jax.ShapeDtypeStruct((8, W, W), BF16),
            jax.ShapeDtypeStruct((8, W, W), BF16),
            jax.ShapeDtypeStruct((1, W), F32),
            jax.ShapeDtypeStruct((1, W), F32),
            jax.ShapeDtypeStruct((1, NP), F32),
        ),
        in_specs=[vmem, vmem, vmem, vmem, vmem, hbm, hbm, vmem],
        out_specs=(hbm, hbm, vmem, vmem, vmem),
        scratch_shapes=scratch,
        compiler_params=pltpu.CompilerParams(
            collective_id=0, has_side_effects=True, vmem_limit_bytes=60 << 20
        ),
    )(
        logged,
        pairs.T,
        clicks.reshape(1, NP),
        query_pairs.T,
        query_clicks.reshape(1, 8),
        first_weight.reshape(16, 2, W, W),
        second_weight.reshape(16, 2, W, W),
        head_weight.reshape(1, W),
    )
    solved = on_gradient * gradient.reshape(8 * W, W).astype(F32) + on_product * product.reshape(8 * W, W).astype(F32)
    return (solved, influence.reshape(NP))


def solution(mesh):
    placed = (
        P("dp", "fsdp"),
        P("dp", None),
        P("dp"),
        P("dp", None),
        P("dp"),
        P(None, "fsdp"),
        P(None, "fsdp"),
        P("fsdp"),
    )
    return jax.shard_map(
        local, mesh=mesh, in_specs=placed, out_specs=(P("dp", "fsdp"), P("dp")), check_vma=False
    )
```

```python
import jax
import jax.numpy as jnp
from jax import lax
from jax.experimental import pallas as pl
from jax.experimental.pallas import tpu as pltpu
from jax.sharding import PartitionSpec as P

DAMPING = 0.01
MESH = pl.DeviceIdType.MESH
F32 = jnp.float32
BF16 = jnp.bfloat16

NP = 128
NQ = 16
HALF = (144, 128)
W = 256
SPLIT_A = 6
SPLIT_B = 6


def dot(left, right):
    return jnp.dot(left, right, preferred_element_type=F32)


def dot_nt(left, right):
    return lax.dot_general(left, right, (((1,), (1,)), ((), ())), preferred_element_type=F32)


def kernel(
    logged, pairs, clicks, qpairs, qclicks, w1, w2, head,
    g_out, p_out, on_g, on_p, infl,
    F0, F1, H0, H1, W1o, W1s, W2o, W2s,
    Ao0, Ao1, As0, As1, Ar0, Ar1, Bo0, Bo1, Bs0, Bs1, Br0, Br1,
    Co0, Co1, Cs0, Cs1, Pb0, Pb1, RB0, RB1, Sa0, Sa1, RA0, RA1,
    Fz0, Fz1, FT, FU, KT, MX, QA, SC, SCr, SP, SPr, SZ, Gp, Pp, R0,
    AR, ARr, ARp, ARpr, ARz,
    loc, wsnd, wrcv, asnd, arcv, bsnd, brcv, csnd, crcv, dsnd, drcv, fsnd, frcv, gsnd, grcv,
    ksnd, krcv, msnd, mrcv, ssnd, srcv, rsnd, rrcv,
):
    F, H = (F0, F1), (H0, H1)
    Ao, As, Ar = (Ao0, Ao1), (As0, As1), (Ar0, Ar1)
    Bo, Bs, Br = (Bo0, Bo1), (Bs0, Bs1), (Br0, Br1)
    Co, Cs = (Co0, Co1), (Cs0, Cs1)
    Pb, RB, Sa, RA = (Pb0, Pb1), (RB0, RB1), (Sa0, Sa1), (RA0, RA1)
    Fz = (Fz0, Fz1)

    z = lax.axis_index("dp")
    f = lax.axis_index("fsdp")
    c = lax.rem(f, 2)
    me = lax.div(f, 2)
    x = lax.rem(me, 4)
    y = lax.div(me, 4)

    def plane(da, db):
        nx = lax.rem(x + da * (1 - c) + db * c + 8, 4)
        ny = lax.rem(y + da * c + db * (1 - c) + 8, 4)
        return ny * 4 + nx

    def dev(da, db):
        return (z, plane(da, db) * 2 + c)

    def zdev(dz):
        return (lax.rem(z + dz + 4, 4), f)

    sibling = (z, me * 2 + 1 - c)
    offsets = [(da, db) for da in range(4) for db in range(4) if (da, db) != (0, 0)]
    partners = [sibling] + [dev(d, 0) for d in (1, 2, 3)] + [dev(0, d) for d in (1, 2, 3)] + [zdev(d) for d in (1, 2, 3)]
    barrier = pltpu.get_barrier_semaphore()
    for partner in partners:
        pl.semaphore_signal(barrier, inc=1, device_id=partner, device_id_type=MESH)

    sent = []

    def remote(src, dst, send_sem, recv_sem, device):
        return pltpu.make_async_remote_copy(
            src_ref=src, dst_ref=dst, send_sem=send_sem, recv_sem=recv_sem,
            device_id=device, device_id_type=MESH,
        )

    def push(src, dst, send_sem, recv_sem, device):
        copy = remote(src, dst, send_sem, recv_sem, device)
        copy.start()
        sent.append(copy)
        return copy

    rows128 = lax.broadcasted_iota(jnp.int32, (128, 128), 0)
    lanes128 = lax.broadcasted_iota(jnp.int32, (128, 128), 1)
    eye = rows128 == lanes128

    def to_row(column):
        return jnp.sum(jnp.where(eye, jnp.broadcast_to(column, (128, 128)), 0.0), axis=0, keepdims=True)

    def to_column(row):
        return jnp.sum(jnp.where(eye, jnp.broadcast_to(row, (128, 128)), 0.0), axis=1, keepdims=True)

    w1_own = pltpu.make_async_copy(w1.at[:, c], W1o, loc.at[0])
    w2_own = pltpu.make_async_copy(w2.at[:, c], W2o, loc.at[1])
    w1_own.start()

    def select(row, count):
        lanes = lax.broadcasted_iota(jnp.int32, (128, 512), 1)
        ids = to_column(row.astype(F32)).astype(jnp.int32)
        return dot((ids == lanes).astype(F32).astype(BF16)[0:count], logged[...]).astype(BF16)

    F0[me, 0:NP] = select(pairs[0:1], NP)
    query_ids = jnp.concatenate([qpairs[0:1], qpairs[1:2], jnp.zeros((1, 112), jnp.int32)], axis=1)
    F0[me, NP:144] = select(query_ids, NQ)
    F1[me] = select(pairs[1:2], NP)
    pl.semaphore_wait(barrier, len(partners))
    w1_sib = push(w1.at[:, 1 - c], W1s, wsnd.at[0], wrcv.at[0], sibling)

    def gather_send(h, buf, snd, rcv):
        first = {}
        for d in (2, 1, 3):
            first[d] = push(buf[h].at[me], buf[h].at[me], snd.at[h, d - 1], rcv.at[h, d - 1], dev(d, 0))
        return first

    def gather_across(h, buf, snd, rcv):
        for e in (2, 1, 3):
            push(buf[h].at[me], buf[h].at[me], snd.at[h, 2 + e], rcv.at[h, 2 + e], dev(0, e))

    def gather_forward(h, buf, snd, rcv, first):
        for d in (1, 3, 2):
            first[d].wait_recv()
            slot = plane(-d, 0)
            for e in (2, 1, 3):
                i = 3 * d + 2 + e
                push(buf[h].at[slot], buf[h].at[slot], snd.at[h, i], rcv.at[h, i], dev(0, e))

    def matmul_head(h, buf, wo, ws, acc_o, acc_s):
        block = buf[h][me]
        acc_o[h][...] = dot(block, wo[me])
        acc_s[h][...] = dot(block, ws[me])

        @pl.loop(1, 4)
        def _(d):
            slot = plane(-d, 0)
            block = buf[h][slot]
            acc_o[h][...] += dot(block, wo[slot])
            acc_s[h][...] += dot(block, ws[slot])

    def matmul_tail(h, buf, wo, ws, acc_o, acc_s, snd, rcv, start, stop):
        @pl.loop(start, stop)
        def _(i):
            slot = plane(-lax.div(i, 3), -(lax.rem(i, 3) + 1))
            remote(buf[h].at[slot], buf[h].at[slot], snd.at[h, 3 + i], rcv.at[h, 3 + i], sibling).wait_recv()
            block = buf[h][slot]
            acc_o[h][...] += dot(block, wo[slot])
            acc_s[h][...] += dot(block, ws[slot])

    first0 = gather_send(0, F, asnd, arcv)
    gather_across(0, F, asnd, arcv)
    first1 = gather_send(1, F, asnd, arcv)
    gather_forward(0, F, asnd, arcv, first0)
    w1_own.wait()
    w1_sib.wait_recv()
    w2_own.start()
    w2_sib = push(w2.at[:, 1 - c], W2s, wsnd.at[1], wrcv.at[1], sibling)

    fz_copies, fz_own, fz_sib = {}, {}, []

    def feature_exchange(h):
        for dz in (1, 3, 2):
            z2 = lax.rem(z + dz, 4)
            fz_copies[h, dz] = push(
                F[h].at[pl.ds(4 * z2, 4)], Fz[h].at[z, c], fsnd.at[h, dz - 1], frcv.at[h, dz - 1], zdev(dz)
            )
        own = F[h].at[pl.ds(4 * z, 4)]
        fz_own[h] = pltpu.make_async_copy(own, Fz[h].at[z, c], loc.at[2 + h])
        fz_own[h].start()
        fz_sib.append(push(own, Fz[h].at[z, c], gsnd.at[h, 0], grcv.at[h, 0], sibling))

    def feature_forward(h):
        for dz in (1, 3, 2):
            fz_copies[h, dz].wait_recv()
            zs = lax.rem(z - dz + 4, 4)
            fz_sib.append(push(Fz[h].at[zs, c], Fz[h].at[zs, c], gsnd.at[h, dz], grcv.at[h, dz], sibling))

    matmul_head(0, F, W1o, W1s, Ao, As)
    matmul_tail(0, F, W1o, W1s, Ao, As, asnd, arcv, 0, SPLIT_A)
    gather_across(1, F, asnd, arcv)
    gather_forward(1, F, asnd, arcv, first1)
    matmul_tail(0, F, W1o, W1s, Ao, As, asnd, arcv, SPLIT_A, 12)
    acc0 = push(As0, Ar0, dsnd.at[0], drcv.at[0], sibling)
    feature_exchange(0)
    matmul_head(1, F, W1o, W1s, Ao, As)
    acc0.wait_recv()
    H0[me] = jnp.tanh(Ao0[...] + Ar0[...]).astype(BF16)
    first0 = gather_send(0, H, bsnd, brcv)
    gather_across(0, H, bsnd, brcv)
    matmul_tail(1, F, W1o, W1s, Ao, As, asnd, arcv, 0, SPLIT_B)
    gather_forward(0, H, bsnd, brcv, first0)
    matmul_tail(1, F, W1o, W1s, Ao, As, asnd, arcv, SPLIT_B, 12)
    acc1 = push(As1, Ar1, dsnd.at[1], drcv.at[1], sibling)
    feature_exchange(1)
    acc1.wait_recv()
    H1[me] = jnp.tanh(Ao1[...] + Ar1[...]).astype(BF16)
    first1 = gather_send(1, H, bsnd, brcv)
    w2_own.wait()
    w2_sib.wait_recv()

    weights = head[...]
    back_copies, coef_copies = {}, {}

    def head_terms(h):
        act = jnp.tanh(Bo[h][...] + Br[h][...])
        Co[h][...] = (weights * (1.0 - act * act)).astype(BF16)
        coef_copies[h] = push(Co[h], Cs[h], dsnd.at[4 + h], drcv.at[4 + h], sibling)
        part = jnp.sum(act * weights, axis=1, keepdims=True)
        SC[h : h + 1] = to_row(part[0:NP])
        if h == 0:
            queries = jnp.concatenate([part[NP:144], jnp.zeros((128 - NQ, 1), F32)], axis=0)
            SC[2:3] = to_row(queries)

    def back_block(h, k):
        return dot_nt(Co[h][...], W2o[k]) + dot_nt(Cs[h][...], W2s[k])

    order = (2, 1, 3, 0)

    def back_send(h):
        coef_copies[h].wait_recv()
        for da in order:
            for e in (2, 1, 3):
                k = plane(da, e)
                Pb[h][k] = back_block(h, k).astype(BF16)
                i = 3 * da + e - 1
                back_copies[h, da, e] = push(
                    Pb[h].at[k], RB[h].at[i], csnd.at[h, i], crcv.at[h, i], dev(0, e)
                )

    def back_own(h):
        for da in order:
            Sa[h][da] = back_block(h, plane(da, 0))

    def back_sum(h):
        for da in order:
            total = Sa[h][da]
            for e in (1, 3, 2):
                back_copies[h, da, e].wait_recv()
                total += RB[h][3 * da + e - 1].astype(F32)
            if da:
                k = plane(da, 0)
                Pb[h][k] = total.astype(BF16)
                back_copies[h, da, 0] = push(
                    Pb[h].at[k], RA[h].at[da - 1], csnd.at[h, 11 + da], crcv.at[h, 11 + da], dev(da, 0)
                )
            else:
                Sa[h][0] = total

    def mixing_of(h):
        total = Sa[h][0]
        for d in (1, 3, 2):
            back_copies[h, d, 0].wait_recv()
            total += RA[h][d - 1].astype(F32)
        own = H[h][me].astype(F32)
        return (1.0 - own * own) * total

    SC[...] = jnp.zeros((8, 128), F32)
    matmul_head(0, H, W2o, W2s, Bo, Bs)
    matmul_tail(0, H, W2o, W2s, Bo, Bs, bsnd, brcv, 0, SPLIT_A)
    gather_across(1, H, bsnd, brcv)
    gather_forward(1, H, bsnd, brcv, first1)
    matmul_tail(0, H, W2o, W2s, Bo, Bs, bsnd, brcv, SPLIT_A, 12)
    acc0 = push(Bs0, Br0, dsnd.at[2], drcv.at[2], sibling)
    matmul_head(1, H, W2o, W2s, Bo, Bs)
    acc0.wait_recv()
    head_terms(0)
    back_send(0)
    matmul_tail(1, H, W2o, W2s, Bo, Bs, bsnd, brcv, 0, 12)
    acc1 = push(Bs1, Br1, dsnd.at[3], drcv.at[3], sibling)
    back_own(0)
    acc1.wait_recv()
    head_terms(1)
    pair = push(SC, SCr, dsnd.at[6], drcv.at[6], sibling)
    back_send(1)
    pair.wait_recv()
    SP[...] = SC[...] + SCr[...]
    scores = [
        push(SP, SPr.at[i], ssnd.at[i], srcv.at[i], dev(da, db)) for i, (da, db) in enumerate(offsets)
    ]
    feature_forward(0)
    back_own(1)
    feature_forward(1)
    back_sum(0)
    fz_own[0].wait()
    fz_own[1].wait()
    for copy in fz_sib:
        copy.wait_recv()

    @pl.loop(0, 8)
    def _(b):
        par, k = lax.rem(b, 2), lax.div(b, 2)
        queries = jnp.concatenate([Fz0[zz, par, k, NP:144] for zz in range(4)], axis=0)
        FU[b] = queries.astype(F32).T.astype(BF16)

    kt = []
    for dz in (2, 1, 3, 0):
        zt = lax.rem(z + dz, 4)
        for h in range(2):
            total = jnp.zeros((NP, 4 * NQ), F32)
            for b in range(8):
                total += dot(Fz[h][zt, b % 2, b // 2, 0:NP], FU[b])
            KT[4 + dz, h] = total
        if dz:
            kt.append(push(KT.at[4 + dz], KT.at[dz], ksnd.at[dz - 1], krcv.at[dz - 1], zdev(dz)))

    back_sum(1)

    score = SP[...]
    for i, copy in enumerate(scores):
        copy.wait_recv()
        score += SPr[i]
    SZ[0] = score
    sz = [push(SZ.at[0], SZ.at[d], ssnd.at[14 + d], srcv.at[14 + d], zdev(d)) for d in (1, 2, 3)]

    mixing = mixing_of(0)
    margin = score[2:3] - pltpu.roll(score[2:3], 120, 1)
    signed = 2.0 * qclicks[...].astype(F32) - 1.0
    slope_query = -signed * jax.nn.sigmoid(-signed * margin[:, 0:8])
    err_row = jnp.concatenate([slope_query, -slope_query, jnp.zeros((1, 112), F32)], axis=1)
    err = to_column(err_row)[0:NQ]
    QA[z] = (err * mixing[NP:144]).astype(BF16)
    qa = [push(QA.at[z], QA.at[z], msnd.at[d - 1], mrcv.at[d - 1], zdev(d)) for d in (1, 2, 3)]
    MX[0, z] = mixing[0:NP].astype(BF16)
    mx = [push(MX.at[0, z], MX.at[0, z], msnd.at[2 + d], mrcv.at[2 + d], zdev(d)) for d in (1, 2, 3)]

    for copy in qa:
        copy.wait_recv()
    squares = jnp.zeros((1, W), F32)
    query_rows = jnp.concatenate([QA[zz] for zz in range(4)], axis=0)
    for b in range(8):
        block = dot(FU[b], query_rows)
        squares += jnp.sum(block * block, axis=0, keepdims=True)
        Gp[b] = block.astype(BF16)
    g_copy = pltpu.make_async_copy(Gp, g_out, loc.at[4])
    g_copy.start()
    norm_part = jnp.broadcast_to(jnp.sum(squares, axis=1, keepdims=True), (8, 128))
    cross_rows = KT[4]
    for copy in kt:
        copy.wait_recv()
    for dz in (1, 2, 3):
        cross_rows += KT[dz]
    cross_rows = cross_rows.astype(BF16)

    second = mixing_of(1)
    MX[1, z] = second.astype(BF16)
    mx += [push(MX.at[1, z], MX.at[1, z], msnd.at[5 + d], mrcv.at[5 + d], zdev(d)) for d in (1, 2, 3)]
    own_response = []
    for h, rows in enumerate((mixing[0:NP], second)):
        project = dot(cross_rows[h], query_rows)
        own_response.append(to_row(jnp.sum(rows * project, axis=1, keepdims=True)))
    replica = lax.broadcasted_iota(jnp.int32, (4, 128), 0) == z
    own_tile = jnp.concatenate(
        [jnp.where(replica, jnp.broadcast_to(row, (4, 128)), 0.0) for row in own_response], axis=0
    )

    def all_reduce(tile, turn, between):
        base = turn * 19
        AR[turn] = tile
        pair = push(AR.at[turn], ARr.at[turn], rsnd.at[base], rrcv.at[base], sibling)
        pair.wait_recv()
        tile = AR[turn] + ARr[turn]
        ARp[turn] = tile
        copies = [
            push(ARp.at[turn], ARpr.at[turn, i], rsnd.at[base + 1 + i], rrcv.at[base + 1 + i], dev(da, db))
            for i, (da, db) in enumerate(offsets)
        ]
        between()
        for i, copy in enumerate(copies):
            copy.wait_recv()
            tile += ARpr[turn, i]
        ARz[turn, 0] = tile
        copies = [
            push(ARz.at[turn, 0], ARz.at[turn, d], rsnd.at[base + 15 + d], rrcv.at[base + 15 + d], zdev(d))
            for d in (1, 2, 3)
        ]
        for d, copy in enumerate(copies):
            copy.wait_recv()
            tile += ARz[turn, d + 1]
        return tile

    def transposes():
        @pl.loop(0, 8)
        def _(b):
            par, k = lax.rem(b, 2), lax.div(b, 2)
            for h in range(2):
                for zz in range(4):
                    at = (4 * h + zz) * NP
                    FT[b, :, at : at + NP] = Fz[h][zz, par, k, 0:NP].T

    tile = all_reduce(jnp.concatenate([own_tile, norm_part], axis=0), 0, transposes)

    for copy in sz:
        copy.wait_recv()
    train_margin = []
    for zz in range(4):
        other = SZ[lax.rem(z - zz + 4, 4)]
        train_margin.append(other[0:1] - other[1:2])
    margins = jnp.concatenate(train_margin, axis=0)
    curve = jax.nn.sigmoid(margins) * jax.nn.sigmoid(-margins)
    for copy in mx:
        copy.wait_recv()

    rdiff_first = tile[0:4] - tile[4:8]
    norm_first = tile[8:9, 0:1]
    resp_err = curve * rdiff_first
    for zz in range(4):
        scale = to_column(resp_err[zz : zz + 1])
        R0[zz * NP : (zz + 1) * NP] = (scale * MX[0, zz].astype(F32)).astype(BF16)
        R0[(4 + zz) * NP : (5 + zz) * NP] = (-scale * MX[1, zz].astype(F32)).astype(BF16)
    for b in range(0, 8, 4):
        rows = FT[b : b + 4].reshape(4 * W, 8 * NP)
        Pp[b : b + 4] = dot(rows, R0[...]).astype(BF16).reshape(4, W, W)
    p_copy = pltpu.make_async_copy(Pp, p_out, loc.at[5])
    p_copy.start()

    response = []
    for h in range(2):
        project = jnp.zeros((4 * NP, W), F32)
        for b in range(8):
            rows = jnp.concatenate([Fz[h][zz, b % 2, b // 2, 0:NP] for zz in range(4)], axis=0)
            project += dot(rows, Pp[b])
        for zz in range(4):
            weighted = MX[h, zz].astype(F32) * project[zz * NP : (zz + 1) * NP]
            response.append(to_row(jnp.sum(weighted, axis=1, keepdims=True)))
    tile = all_reduce(jnp.concatenate(response + [norm_part], axis=0), 1, lambda: None)
    rdiff_prod = tile[0:4] - tile[4:8]

    def total_of(value):
        return jnp.sum(jnp.sum(value, axis=1, keepdims=True), axis=0, keepdims=True)

    cross = total_of(curve * rdiff_first * rdiff_first)
    prod_norm = total_of(curve * rdiff_first * rdiff_prod)
    curv_first = cross + DAMPING * norm_first
    alpha_first = norm_first / curv_first
    keep = 1.0 - DAMPING * alpha_first
    norm_next = keep * keep * norm_first - 2.0 * keep * alpha_first * cross + alpha_first * alpha_first * prod_norm
    lead = keep + norm_next / norm_first
    rdiff_next = lead * rdiff_first - alpha_first * rdiff_prod
    direction_norm = lead * lead * norm_first - 2.0 * lead * alpha_first * cross + alpha_first * alpha_first * prod_norm
    curv_next = total_of(curve * rdiff_next * rdiff_next) + DAMPING * direction_norm
    alpha_next = norm_next / curv_next
    on_gradient = alpha_first + alpha_next * lead
    on_product = -alpha_next * alpha_first

    own_margin = score[0:1] - score[1:2]
    signed = 2.0 * clicks[...].astype(F32) - 1.0
    slope = -signed * jax.nn.sigmoid(-signed * own_margin)
    change = alpha_first * rdiff_first + alpha_next * rdiff_next
    on_g[...] = jnp.broadcast_to(on_gradient, (1, W))
    on_p[...] = jnp.broadcast_to(on_product, (1, W))
    infl[...] = -slope * jnp.sum(jnp.where(replica, change, 0.0), axis=0, keepdims=True)

    g_copy.wait()
    p_copy.wait()
    for copy in sent:
        copy.wait_send()


def local(logged, pairs, clicks, query_pairs, query_clicks, first_weight, second_weight, head_weight):
    vmem = pl.BlockSpec(memory_space=pltpu.VMEM)
    hbm = pl.BlockSpec(memory_space=pl.ANY)
    V = pltpu.VMEM
    dma = pltpu.SemaphoreType.DMA

    def halves(dtype, *lead):
        return [V((*lead, rows, W), dtype) for rows in HALF]

    scratch = (
        halves(BF16, 16) + halves(BF16, 16)
        + [V((16, W, W), BF16)] * 4
        + halves(F32) * 6
        + halves(BF16) * 2
        + halves(BF16, 16) + halves(BF16, 12) + halves(F32, 4) + halves(BF16, 3)
        + halves(BF16, 4, 2, 4)
        + [V((8, W, 8 * NP), BF16), V((8, W, 4 * NQ), BF16)]
        + [V((8, 2, NP, 4 * NQ), F32)]
        + [V((2, 4, NP, W), BF16), V((4, NQ, W), BF16)]
        + [V((8, 128), F32)] * 3 + [V((15, 8, 128), F32), V((4, 8, 128), F32)]
        + [V((8, W, W), BF16)] * 2
        + [V((8 * NP, W), BF16)]
        + [V((2, 16, 128), F32)] * 3 + [V((2, 15, 16, 128), F32), V((2, 4, 16, 128), F32)]
        + [dma((6,))]
        + [dma((2,))] * 2 + [dma((2, 15))] * 6 + [dma((7,))] * 2
        + [dma((2, 3))] * 2 + [dma((2, 4))] * 2 + [dma((3,))] * 2
        + [dma((9,))] * 2 + [dma((18,))] * 2 + [dma((38,))] * 2
    )
    gradient, product, on_gradient, on_product, influence = pl.pallas_call(
        kernel,
        out_shape=(
            jax.ShapeDtypeStruct((8, W, W), BF16),
            jax.ShapeDtypeStruct((8, W, W), BF16),
            jax.ShapeDtypeStruct((1, W), F32),
            jax.ShapeDtypeStruct((1, W), F32),
            jax.ShapeDtypeStruct((1, NP), F32),
        ),
        in_specs=[vmem, vmem, vmem, vmem, vmem, hbm, hbm, vmem],
        out_specs=(hbm, hbm, vmem, vmem, vmem),
        scratch_shapes=scratch,
        compiler_params=pltpu.CompilerParams(
            collective_id=0, has_side_effects=True, vmem_limit_bytes=60 << 20
        ),
    )(
        logged,
        pairs.T,
        clicks.reshape(1, NP),
        query_pairs.T,
        query_clicks.reshape(1, 8),
        first_weight.reshape(16, 2, W, W),
        second_weight.reshape(16, 2, W, W),
        head_weight.reshape(1, W),
    )
    solved = on_gradient * gradient.reshape(8 * W, W).astype(F32) + on_product * product.reshape(8 * W, W).astype(F32)
    return (solved, influence.reshape(NP))


def solution(mesh):
    placed = (
        P("dp", "fsdp"),
        P("dp", None),
        P("dp"),
        P("dp", None),
        P("dp"),
        P(None, "fsdp"),
        P(None, "fsdp"),
        P("fsdp"),
    )
    return jax.shard_map(
        local, mesh=mesh, in_specs=placed, out_specs=(P("dp", "fsdp"), P("dp")), check_vma=False
    )
```

```python
import jax
import jax.numpy as jnp
from jax import lax
from jax.experimental import pallas as pl
from jax.experimental.pallas import tpu as pltpu
from jax.sharding import PartitionSpec as P

DAMPING = 0.01
MESH = pl.DeviceIdType.MESH
F32 = jnp.float32
BF16 = jnp.bfloat16

NP = 128
NQ = 16
HALF = (144, 128)
W = 256
SPLIT_A = 6
SPLIT_B = 6


def dot(left, right):
    return jnp.dot(left, right, preferred_element_type=F32)


def dot_nt(left, right):
    return lax.dot_general(left, right, (((1,), (1,)), ((), ())), preferred_element_type=F32)


def kernel(
    logged, pairs, clicks, qpairs, qclicks, w1, w2, head,
    g_out, p_out, on_g, on_p, infl,
    F0, F1, H0, H1, W1o, W1s, W2o, W2s,
    Ao0, Ao1, As0, As1, Ar0, Ar1, Bo0, Bo1, Bs0, Bs1, Br0, Br1,
    Co0, Co1, Cs0, Cs1, Pb0, Pb1, RB0, RB1, Sa0, Sa1, RA0, RA1,
    Fz0, Fz1, FT, FU, KT, MX, QA, SC, SCr, SP, SPr, SZ, Gp, Pp, R0,
    AR, ARr, ARp, ARpr, ARz,
    loc, wsnd, wrcv, asnd, arcv, bsnd, brcv, csnd, crcv, dsnd, drcv, fsnd, frcv, gsnd, grcv,
    ksnd, krcv, msnd, mrcv, ssnd, srcv, rsnd, rrcv,
):
    F, H = (F0, F1), (H0, H1)
    Ao, As, Ar = (Ao0, Ao1), (As0, As1), (Ar0, Ar1)
    Bo, Bs, Br = (Bo0, Bo1), (Bs0, Bs1), (Br0, Br1)
    Co, Cs = (Co0, Co1), (Cs0, Cs1)
    Pb, RB, Sa, RA = (Pb0, Pb1), (RB0, RB1), (Sa0, Sa1), (RA0, RA1)
    Fz = (Fz0, Fz1)

    z = lax.axis_index("dp")
    f = lax.axis_index("fsdp")
    c = lax.rem(f, 2)
    me = lax.div(f, 2)
    x = lax.rem(me, 4)
    y = lax.div(me, 4)

    def plane(da, db):
        nx = lax.rem(x + da * (1 - c) + db * c + 8, 4)
        ny = lax.rem(y + da * c + db * (1 - c) + 8, 4)
        return ny * 4 + nx

    def dev(da, db):
        return (z, plane(da, db) * 2 + c)

    def zdev(dz):
        return (lax.rem(z + dz + 4, 4), f)

    sibling = (z, me * 2 + 1 - c)
    offsets = [(da, db) for da in range(4) for db in range(4) if (da, db) != (0, 0)]
    partners = [sibling] + [dev(d, 0) for d in (1, 2, 3)] + [dev(0, d) for d in (1, 2, 3)] + [zdev(d) for d in (1, 2, 3)]
    barrier = pltpu.get_barrier_semaphore()
    for partner in partners:
        pl.semaphore_signal(barrier, inc=1, device_id=partner, device_id_type=MESH)

    sent = []

    def remote(src, dst, send_sem, recv_sem, device):
        return pltpu.make_async_remote_copy(
            src_ref=src, dst_ref=dst, send_sem=send_sem, recv_sem=recv_sem,
            device_id=device, device_id_type=MESH,
        )

    def push(src, dst, send_sem, recv_sem, device):
        copy = remote(src, dst, send_sem, recv_sem, device)
        copy.start()
        sent.append(copy)
        return copy

    rows128 = lax.broadcasted_iota(jnp.int32, (128, 128), 0)
    lanes128 = lax.broadcasted_iota(jnp.int32, (128, 128), 1)
    eye = rows128 == lanes128

    def to_row(column):
        return jnp.sum(jnp.where(eye, jnp.broadcast_to(column, (128, 128)), 0.0), axis=0, keepdims=True)

    def to_column(row):
        return jnp.sum(jnp.where(eye, jnp.broadcast_to(row, (128, 128)), 0.0), axis=1, keepdims=True)

    w1_own = pltpu.make_async_copy(w1.at[:, c], W1o, loc.at[0])
    w2_own = pltpu.make_async_copy(w2.at[:, c], W2o, loc.at[1])
    w1_own.start()

    def select(row, count):
        lanes = lax.broadcasted_iota(jnp.int32, (128, 512), 1)
        ids = to_column(row.astype(F32)).astype(jnp.int32)
        return dot((ids == lanes).astype(F32).astype(BF16)[0:count], logged[...]).astype(BF16)

    F0[me, 0:NP] = select(pairs[0:1], NP)
    query_ids = jnp.concatenate([qpairs[0:1], qpairs[1:2], jnp.zeros((1, 112), jnp.int32)], axis=1)
    F0[me, NP:144] = select(query_ids, NQ)
    F1[me] = select(pairs[1:2], NP)
    pl.semaphore_wait(barrier, len(partners))
    w1_sib = push(w1.at[:, 1 - c], W1s, wsnd.at[0], wrcv.at[0], sibling)

    def gather_send(h, buf, snd, rcv):
        first = {}
        for d in (2, 1, 3):
            first[d] = push(buf[h].at[me], buf[h].at[me], snd.at[h, d - 1], rcv.at[h, d - 1], dev(d, 0))
        return first

    def gather_across(h, buf, snd, rcv):
        for e in (2, 1, 3):
            push(buf[h].at[me], buf[h].at[me], snd.at[h, 2 + e], rcv.at[h, 2 + e], dev(0, e))

    def gather_forward(h, buf, snd, rcv, first):
        for d in (1, 3, 2):
            first[d].wait_recv()
            slot = plane(-d, 0)
            for e in (2, 1, 3):
                i = 3 * d + 2 + e
                push(buf[h].at[slot], buf[h].at[slot], snd.at[h, i], rcv.at[h, i], dev(0, e))

    def matmul_head(h, buf, wo, ws, acc_o, acc_s):
        block = buf[h][me]
        acc_o[h][...] = dot(block, wo[me])
        acc_s[h][...] = dot(block, ws[me])

        @pl.loop(1, 4)
        def _(d):
            slot = plane(-d, 0)
            block = buf[h][slot]
            acc_o[h][...] += dot(block, wo[slot])
            acc_s[h][...] += dot(block, ws[slot])

    def matmul_tail(h, buf, wo, ws, acc_o, acc_s, snd, rcv, start, stop):
        @pl.loop(start, stop)
        def _(i):
            slot = plane(-lax.div(i, 3), -(lax.rem(i, 3) + 1))
            remote(buf[h].at[slot], buf[h].at[slot], snd.at[h, 3 + i], rcv.at[h, 3 + i], sibling).wait_recv()
            block = buf[h][slot]
            acc_o[h][...] += dot(block, wo[slot])
            acc_s[h][...] += dot(block, ws[slot])

    first0 = gather_send(0, F, asnd, arcv)
    gather_across(0, F, asnd, arcv)
    first1 = gather_send(1, F, asnd, arcv)
    gather_forward(0, F, asnd, arcv, first0)
    w1_own.wait()
    w1_sib.wait_recv()
    w2_own.start()
    w2_sib = push(w2.at[:, 1 - c], W2s, wsnd.at[1], wrcv.at[1], sibling)

    fz_copies, fz_own, fz_sib = {}, {}, []

    def feature_exchange(h):
        for dz in (1, 3, 2):
            z2 = lax.rem(z + dz, 4)
            fz_copies[h, dz] = push(
                F[h].at[pl.ds(4 * z2, 4)], Fz[h].at[z, c], fsnd.at[h, dz - 1], frcv.at[h, dz - 1], zdev(dz)
            )
        own = F[h].at[pl.ds(4 * z, 4)]
        fz_own[h] = pltpu.make_async_copy(own, Fz[h].at[z, c], loc.at[2 + h])
        fz_own[h].start()
        fz_sib.append(push(own, Fz[h].at[z, c], gsnd.at[h, 0], grcv.at[h, 0], sibling))

    def feature_forward(h):
        for dz in (1, 3, 2):
            fz_copies[h, dz].wait_recv()
            zs = lax.rem(z - dz + 4, 4)
            fz_sib.append(push(Fz[h].at[zs, c], Fz[h].at[zs, c], gsnd.at[h, dz], grcv.at[h, dz], sibling))

    matmul_head(0, F, W1o, W1s, Ao, As)
    matmul_tail(0, F, W1o, W1s, Ao, As, asnd, arcv, 0, SPLIT_A)
    gather_across(1, F, asnd, arcv)
    gather_forward(1, F, asnd, arcv, first1)
    matmul_tail(0, F, W1o, W1s, Ao, As, asnd, arcv, SPLIT_A, 12)
    acc0 = push(As0, Ar0, dsnd.at[0], drcv.at[0], sibling)
    feature_exchange(0)
    matmul_head(1, F, W1o, W1s, Ao, As)
    acc0.wait_recv()
    H0[me] = jnp.tanh(Ao0[...] + Ar0[...]).astype(BF16)
    first0 = gather_send(0, H, bsnd, brcv)
    gather_across(0, H, bsnd, brcv)
    matmul_tail(1, F, W1o, W1s, Ao, As, asnd, arcv, 0, SPLIT_B)
    gather_forward(0, H, bsnd, brcv, first0)
    matmul_tail(1, F, W1o, W1s, Ao, As, asnd, arcv, SPLIT_B, 12)
    acc1 = push(As1, Ar1, dsnd.at[1], drcv.at[1], sibling)
    feature_exchange(1)
    acc1.wait_recv()
    H1[me] = jnp.tanh(Ao1[...] + Ar1[...]).astype(BF16)
    first1 = gather_send(1, H, bsnd, brcv)
    w2_own.wait()
    w2_sib.wait_recv()

    weights = head[...]
    back_copies, coef_copies = {}, {}

    def head_terms(h):
        act = jnp.tanh(Bo[h][...] + Br[h][...])
        Co[h][...] = (weights * (1.0 - act * act)).astype(BF16)
        coef_copies[h] = push(Co[h], Cs[h], dsnd.at[4 + h], drcv.at[4 + h], sibling)
        part = jnp.sum(act * weights, axis=1, keepdims=True)
        SC[h : h + 1] = to_row(part[0:NP])
        if h == 0:
            queries = jnp.concatenate([part[NP:144], jnp.zeros((128 - NQ, 1), F32)], axis=0)
            SC[2:3] = to_row(queries)

    def back_block(h, k):
        return dot_nt(Co[h][...], W2o[k]) + dot_nt(Cs[h][...], W2s[k])

    order = (2, 1, 3, 0)

    def back_send(h):
        coef_copies[h].wait_recv()
        for da in order:
            for e in (2, 1, 3):
                k = plane(da, e)
                Pb[h][k] = back_block(h, k).astype(BF16)
                i = 3 * da + e - 1
                back_copies[h, da, e] = push(
                    Pb[h].at[k], RB[h].at[i], csnd.at[h, i], crcv.at[h, i], dev(0, e)
                )

    def back_own(h):
        for da in order:
            Sa[h][da] = back_block(h, plane(da, 0))

    def back_sum(h):
        for da in order:
            total = Sa[h][da]
            for e in (1, 3, 2):
                back_copies[h, da, e].wait_recv()
                total += RB[h][3 * da + e - 1].astype(F32)
            if da:
                k = plane(da, 0)
                Pb[h][k] = total.astype(BF16)
                back_copies[h, da, 0] = push(
                    Pb[h].at[k], RA[h].at[da - 1], csnd.at[h, 11 + da], crcv.at[h, 11 + da], dev(da, 0)
                )
            else:
                Sa[h][0] = total

    def mixing_of(h):
        total = Sa[h][0]
        for d in (1, 3, 2):
            back_copies[h, d, 0].wait_recv()
            total += RA[h][d - 1].astype(F32)
        own = H[h][me].astype(F32)
        return (1.0 - own * own) * total

    SC[...] = jnp.zeros((8, 128), F32)
    matmul_head(0, H, W2o, W2s, Bo, Bs)
    matmul_tail(0, H, W2o, W2s, Bo, Bs, bsnd, brcv, 0, SPLIT_A)
    gather_across(1, H, bsnd, brcv)
    gather_forward(1, H, bsnd, brcv, first1)
    matmul_tail(0, H, W2o, W2s, Bo, Bs, bsnd, brcv, SPLIT_A, 12)
    acc0 = push(Bs0, Br0, dsnd.at[2], drcv.at[2], sibling)
    matmul_head(1, H, W2o, W2s, Bo, Bs)
    acc0.wait_recv()
    head_terms(0)
    back_send(0)
    matmul_tail(1, H, W2o, W2s, Bo, Bs, bsnd, brcv, 0, 12)
    acc1 = push(Bs1, Br1, dsnd.at[3], drcv.at[3], sibling)
    acc1.wait_recv()
    head_terms(1)
    pair = push(SC, SCr, dsnd.at[6], drcv.at[6], sibling)
    back_own(0)
    back_send(1)
    pair.wait_recv()
    SP[...] = SC[...] + SCr[...]
    scores = [
        push(SP, SPr.at[i], ssnd.at[i], srcv.at[i], dev(da, db)) for i, (da, db) in enumerate(offsets)
    ]
    feature_forward(0)
    back_own(1)
    feature_forward(1)
    back_sum(0)
    fz_own[0].wait()
    fz_own[1].wait()
    for copy in fz_sib:
        copy.wait_recv()

    @pl.loop(0, 8)
    def _(b):
        par, k = lax.rem(b, 2), lax.div(b, 2)
        queries = jnp.concatenate([Fz0[zz, par, k, NP:144] for zz in range(4)], axis=0)
        FU[b] = queries.astype(F32).T.astype(BF16)

    kt = []
    for dz in (2, 1, 3, 0):
        zt = lax.rem(z + dz, 4)
        for h in range(2):
            total = jnp.zeros((NP, 4 * NQ), F32)
            for b in range(8):
                total += dot(Fz[h][zt, b % 2, b // 2, 0:NP], FU[b])
            KT[4 + dz, h] = total
        if dz:
            kt.append(push(KT.at[4 + dz], KT.at[dz], ksnd.at[dz - 1], krcv.at[dz - 1], zdev(dz)))

    back_sum(1)

    score = SP[...]
    for i, copy in enumerate(scores):
        copy.wait_recv()
        score += SPr[i]
    SZ[0] = score
    sz = [push(SZ.at[0], SZ.at[d], ssnd.at[14 + d], srcv.at[14 + d], zdev(d)) for d in (1, 2, 3)]

    mixing = mixing_of(0)
    margin = score[2:3] - pltpu.roll(score[2:3], 120, 1)
    signed = 2.0 * qclicks[...].astype(F32) - 1.0
    slope_query = -signed * jax.nn.sigmoid(-signed * margin[:, 0:8])
    err_row = jnp.concatenate([slope_query, -slope_query, jnp.zeros((1, 112), F32)], axis=1)
    err = to_column(err_row)[0:NQ]
    QA[z] = (err * mixing[NP:144]).astype(BF16)
    qa = [push(QA.at[z], QA.at[z], msnd.at[d - 1], mrcv.at[d - 1], zdev(d)) for d in (1, 2, 3)]
    MX[0, z] = mixing[0:NP].astype(BF16)
    mx = [push(MX.at[0, z], MX.at[0, z], msnd.at[2 + d], mrcv.at[2 + d], zdev(d)) for d in (1, 2, 3)]

    for copy in qa:
        copy.wait_recv()
    squares = jnp.zeros((1, W), F32)
    query_rows = jnp.concatenate([QA[zz] for zz in range(4)], axis=0)
    for b in range(8):
        block = dot(FU[b], query_rows)
        squares += jnp.sum(block * block, axis=0, keepdims=True)
        Gp[b] = block.astype(BF16)
    g_copy = pltpu.make_async_copy(Gp, g_out, loc.at[4])
    g_copy.start()
    norm_part = jnp.broadcast_to(jnp.sum(squares, axis=1, keepdims=True), (8, 128))
    cross_rows = KT[4]
    for copy in kt:
        copy.wait_recv()
    for dz in (1, 2, 3):
        cross_rows += KT[dz]
    cross_rows = cross_rows.astype(BF16)

    second = mixing_of(1)
    MX[1, z] = second.astype(BF16)
    mx += [push(MX.at[1, z], MX.at[1, z], msnd.at[5 + d], mrcv.at[5 + d], zdev(d)) for d in (1, 2, 3)]
    own_response = []
    for h, rows in enumerate((mixing[0:NP], second)):
        project = dot(cross_rows[h], query_rows)
        own_response.append(to_row(jnp.sum(rows * project, axis=1, keepdims=True)))
    replica = lax.broadcasted_iota(jnp.int32, (4, 128), 0) == z
    own_tile = jnp.concatenate(
        [jnp.where(replica, jnp.broadcast_to(row, (4, 128)), 0.0) for row in own_response], axis=0
    )

    def all_reduce(tile, turn, between):
        base = turn * 19
        AR[turn] = tile
        pair = push(AR.at[turn], ARr.at[turn], rsnd.at[base], rrcv.at[base], sibling)
        pair.wait_recv()
        tile = AR[turn] + ARr[turn]
        ARp[turn] = tile
        copies = [
            push(ARp.at[turn], ARpr.at[turn, i], rsnd.at[base + 1 + i], rrcv.at[base + 1 + i], dev(da, db))
            for i, (da, db) in enumerate(offsets)
        ]
        between()
        for i, copy in enumerate(copies):
            copy.wait_recv()
            tile += ARpr[turn, i]
        ARz[turn, 0] = tile
        copies = [
            push(ARz.at[turn, 0], ARz.at[turn, d], rsnd.at[base + 15 + d], rrcv.at[base + 15 + d], zdev(d))
            for d in (1, 2, 3)
        ]
        for d, copy in enumerate(copies):
            copy.wait_recv()
            tile += ARz[turn, d + 1]
        return tile

    def transposes():
        @pl.loop(0, 8)
        def _(b):
            par, k = lax.rem(b, 2), lax.div(b, 2)
            for h in range(2):
                for zz in range(4):
                    at = (4 * h + zz) * NP
                    FT[b, :, at : at + NP] = Fz[h][zz, par, k, 0:NP].T

    tile = all_reduce(jnp.concatenate([own_tile, norm_part], axis=0), 0, transposes)

    for copy in sz:
        copy.wait_recv()
    train_margin = []
    for zz in range(4):
        other = SZ[lax.rem(z - zz + 4, 4)]
        train_margin.append(other[0:1] - other[1:2])
    margins = jnp.concatenate(train_margin, axis=0)
    curve = jax.nn.sigmoid(margins) * jax.nn.sigmoid(-margins)
    for copy in mx:
        copy.wait_recv()

    rdiff_first = tile[0:4] - tile[4:8]
    norm_first = tile[8:9, 0:1]
    resp_err = curve * rdiff_first
    for zz in range(4):
        scale = to_column(resp_err[zz : zz + 1])
        R0[zz * NP : (zz + 1) * NP] = (scale * MX[0, zz].astype(F32)).astype(BF16)
        R0[(4 + zz) * NP : (5 + zz) * NP] = (-scale * MX[1, zz].astype(F32)).astype(BF16)
    for b in range(0, 8, 4):
        rows = FT[b : b + 4].reshape(4 * W, 8 * NP)
        Pp[b : b + 4] = dot(rows, R0[...]).astype(BF16).reshape(4, W, W)
    p_copy = pltpu.make_async_copy(Pp, p_out, loc.at[5])
    p_copy.start()

    response = []
    for h in range(2):
        project = jnp.zeros((4 * NP, W), F32)
        for b in range(8):
            rows = jnp.concatenate([Fz[h][zz, b % 2, b // 2, 0:NP] for zz in range(4)], axis=0)
            project += dot(rows, Pp[b])
        for zz in range(4):
            weighted = MX[h, zz].astype(F32) * project[zz * NP : (zz + 1) * NP]
            response.append(to_row(jnp.sum(weighted, axis=1, keepdims=True)))
    tile = all_reduce(jnp.concatenate(response + [norm_part], axis=0), 1, lambda: None)
    rdiff_prod = tile[0:4] - tile[4:8]

    def total_of(value):
        return jnp.sum(jnp.sum(value, axis=1, keepdims=True), axis=0, keepdims=True)

    cross = total_of(curve * rdiff_first * rdiff_first)
    prod_norm = total_of(curve * rdiff_first * rdiff_prod)
    curv_first = cross + DAMPING * norm_first
    alpha_first = norm_first / curv_first
    keep = 1.0 - DAMPING * alpha_first
    norm_next = keep * keep * norm_first - 2.0 * keep * alpha_first * cross + alpha_first * alpha_first * prod_norm
    lead = keep + norm_next / norm_first
    rdiff_next = lead * rdiff_first - alpha_first * rdiff_prod
    direction_norm = lead * lead * norm_first - 2.0 * lead * alpha_first * cross + alpha_first * alpha_first * prod_norm
    curv_next = total_of(curve * rdiff_next * rdiff_next) + DAMPING * direction_norm
    alpha_next = norm_next / curv_next
    on_gradient = alpha_first + alpha_next * lead
    on_product = -alpha_next * alpha_first

    own_margin = score[0:1] - score[1:2]
    signed = 2.0 * clicks[...].astype(F32) - 1.0
    slope = -signed * jax.nn.sigmoid(-signed * own_margin)
    change = alpha_first * rdiff_first + alpha_next * rdiff_next
    on_g[...] = jnp.broadcast_to(on_gradient, (1, W))
    on_p[...] = jnp.broadcast_to(on_product, (1, W))
    infl[...] = -slope * jnp.sum(jnp.where(replica, change, 0.0), axis=0, keepdims=True)

    g_copy.wait()
    p_copy.wait()
    for copy in sent:
        copy.wait_send()


def local(logged, pairs, clicks, query_pairs, query_clicks, first_weight, second_weight, head_weight):
    vmem = pl.BlockSpec(memory_space=pltpu.VMEM)
    hbm = pl.BlockSpec(memory_space=pl.ANY)
    V = pltpu.VMEM
    dma = pltpu.SemaphoreType.DMA

    def halves(dtype, *lead):
        return [V((*lead, rows, W), dtype) for rows in HALF]

    scratch = (
        halves(BF16, 16) + halves(BF16, 16)
        + [V((16, W, W), BF16)] * 4
        + halves(F32) * 6
        + halves(BF16) * 2
        + halves(BF16, 16) + halves(BF16, 12) + halves(F32, 4) + halves(BF16, 3)
        + halves(BF16, 4, 2, 4)
        + [V((8, W, 8 * NP), BF16), V((8, W, 4 * NQ), BF16)]
        + [V((8, 2, NP, 4 * NQ), F32)]
        + [V((2, 4, NP, W), BF16), V((4, NQ, W), BF16)]
        + [V((8, 128), F32)] * 3 + [V((15, 8, 128), F32), V((4, 8, 128), F32)]
        + [V((8, W, W), BF16)] * 2
        + [V((8 * NP, W), BF16)]
        + [V((2, 16, 128), F32)] * 3 + [V((2, 15, 16, 128), F32), V((2, 4, 16, 128), F32)]
        + [dma((6,))]
        + [dma((2,))] * 2 + [dma((2, 15))] * 6 + [dma((7,))] * 2
        + [dma((2, 3))] * 2 + [dma((2, 4))] * 2 + [dma((3,))] * 2
        + [dma((9,))] * 2 + [dma((18,))] * 2 + [dma((38,))] * 2
    )
    gradient, product, on_gradient, on_product, influence = pl.pallas_call(
        kernel,
        out_shape=(
            jax.ShapeDtypeStruct((8, W, W), BF16),
            jax.ShapeDtypeStruct((8, W, W), BF16),
            jax.ShapeDtypeStruct((1, W), F32),
            jax.ShapeDtypeStruct((1, W), F32),
            jax.ShapeDtypeStruct((1, NP), F32),
        ),
        in_specs=[vmem, vmem, vmem, vmem, vmem, hbm, hbm, vmem],
        out_specs=(hbm, hbm, vmem, vmem, vmem),
        scratch_shapes=scratch,
        compiler_params=pltpu.CompilerParams(
            collective_id=0, has_side_effects=True, vmem_limit_bytes=60 << 20
        ),
    )(
        logged,
        pairs.T,
        clicks.reshape(1, NP),
        query_pairs.T,
        query_clicks.reshape(1, 8),
        first_weight.reshape(16, 2, W, W),
        second_weight.reshape(16, 2, W, W),
        head_weight.reshape(1, W),
    )
    solved = on_gradient * gradient.reshape(8 * W, W).astype(F32) + on_product * product.reshape(8 * W, W).astype(F32)
    return (solved, influence.reshape(NP))


def solution(mesh):
    placed = (
        P("dp", "fsdp"),
        P("dp", None),
        P("dp"),
        P("dp", None),
        P("dp"),
        P(None, "fsdp"),
        P(None, "fsdp"),
        P("fsdp"),
    )
    return jax.shard_map(
        local, mesh=mesh, in_specs=placed, out_specs=(P("dp", "fsdp"), P("dp")), check_vma=False
    )
```
